1024 devices in a mesh: worker: 8 (over y, x_lo), fsdp: 128 (over x_hi, z, core).
Axes of the slice: x: 4 (x_hi: 2, x_lo: 2; x = x_hi * 2 + x_lo), y: 4, z: 32, core: 2. Of those that a mesh axis runs over, the one named last changes fastest.
Arguments:
- params: float32 [8, 4096, 128], P('worker', 'fsdp'), may hold values from -6 to 6
- first_moment: float32 [8, 4096, 128], P('worker', 'fsdp'), may hold values from -4 to 4
- second_moment: float32 [8, 4096, 128], P('worker', 'fsdp'), may hold values from 0.05 to 2
- global_fragment: float32 [1024, 128], P('fsdp'), may hold values from -6 to 6
- outer_momentum: float32 [1024, 128], P('fsdp'), may hold values from -6 to 6
- features: bfloat16 [8, 16384, 4096], P('worker', 'fsdp'), may hold values from -6 to 6
- cotangent: bfloat16 [8, 16384, 128], P('worker', 'fsdp'), may hold values from -768 to 768
- token_counts: int32 [8], replicated, may hold values from 2048 to 16384
- fragment_index: int32 [1], replicated, may hold values from 0 to 3
Outputs:
- new_params: float32 [8, 4096, 128], P('worker', 'fsdp')
- new_first: float32 [8, 4096, 128], P('worker', 'fsdp')
- new_second: float32 [8, 4096, 128], P('worker', 'fsdp')
- new_global: float32 [1024, 128], P('fsdp')
- new_momentum: float32 [1024, 128], P('fsdp')
The draws below stay inside these ranges and needn't reach their ends.
All inputs are finite; a program needn't handle non-finite values.
Results may differ from the reference program's by a relative error of at most 0.0003.
Values sent between devices are 32-bit elements; how exact they have to be, the bound alone decides.
A program may use at most 32 MiB of HBM per device.

```python
import math
import jax
import jax.numpy as jnp
from jax import lax

D = 4096
KVW = 128
FRAGS = 4
TOK_W = 16384
WORKERS = 8
FROWS = 1024


def touch_ends(entries, rng, smallest, high):
    longest = entries.shape.index(max(entries.shape))
    spots = []
    for shift in (0, 1):
        where = [jax.random.randint(jax.random.fold_in(rng, axis), (), 0, length) for axis, length in enumerate(entries.shape)]
        where[longest] = (where[longest] + shift) % entries.shape[longest]
        spots.append(tuple(where))
    return entries.at[spots[0]].set(smallest).at[spots[1]].set(high)


def block_levels(own_key, extent, shards, least, largest):
    def one(axis_at, shards_of):
        draws = jax.random.uniform(jax.random.fold_in(jax.random.fold_in(own_key, 6), axis_at), (shards_of,), jnp.float32, least / len(shards), largest / len(shards))
        return jnp.repeat(jnp.exp(draws), extent[axis_at] // shards_of).reshape((-1,) + (1,) * (len(extent) - axis_at - 1))

    factor_of = one(*shards[0])
    for cut in shards[1:]:
        factor_of = factor_of * one(*cut)
    return factor_of


def bell_draw(own_key, shape, scale, bound, cuts=(), kind=jnp.bfloat16):
    entries = scale * jax.random.normal(own_key, shape, jnp.float32)
    if cuts:
        entries = entries * block_levels(own_key, shape, cuts, -0.22, 0.18)
    return jnp.clip(entries, -bound, bound).astype(kind)


def setup_inputs(seed: int = 0) -> dict:
    keys = jax.random.split(jax.random.key(seed), 10)
    return {
        "params": bell_draw(keys[0], (WORKERS, D, KVW), 1.0, 6.0, ((0, 8), (1, 128)), jnp.float32),
        "first_moment": bell_draw(keys[1], (WORKERS, D, KVW), 0.3, 4.0, ((0, 8), (1, 128)), jnp.float32),
        "second_moment": jnp.clip(jnp.exp(math.log(2.0) - 3.6888794 * jax.random.uniform(keys[2], (WORKERS, D, KVW), jnp.float32) ** block_levels(keys[2], (WORKERS, D, KVW), ((0, 8), (1, 128)), -0.2, 0.2)), 0.05, 2.0),
        "global_fragment": bell_draw(keys[3], (FROWS, KVW), 1.0, 6.0, ((0, 128),), jnp.float32),
        "outer_momentum": bell_draw(keys[4], (FROWS, KVW), 0.5, 6.0, ((0, 128),), jnp.float32),
        "features": bell_draw(keys[5], (WORKERS, TOK_W, D), 1.0, 6.0, ((0, 8), (1, 128))),
        "cotangent": bell_draw(keys[6], (WORKERS, TOK_W, KVW), (TOK_W ** 0.5), 768.0, ((0, 8), (1, 128))),
        "token_counts": touch_ends(jax.random.randint(keys[7], (WORKERS,), TOK_W // 8, TOK_W + 1), jax.random.fold_in(keys[7], 1), TOK_W // 8, TOK_W).astype(jnp.int32),
        "fragment_index": jax.random.randint(keys[8], (1,), 0, FRAGS).astype(jnp.int32),
    }


BETA_ONE = 0.9
BETA_TWO = 0.95
CORRECT_ONE = 0.6513216
CORRECT_TWO = 0.401263
ADAM_EPS = 1e-08
LEARN_RATE = 0.02
DECAY_RATE = 0.1
NESTEROV = 0.9
OUTER_RATE = 0.7
MIXING = 0.5

def reference(params, first_moment, second_moment, global_fragment, outer_momentum, features, cotangent, token_counts, fragment_index):
    fragment = fragment_index[0].astype(jnp.int32)
    token_total = jnp.sum(token_counts).astype(jnp.float32)
    positions = jnp.arange(TOK_W, dtype=jnp.int32)
    drift_sum = jnp.zeros((FROWS, KVW), jnp.float32)
    inner_list, first_list, second_list = ([], [], [])
    for worker in range(WORKERS):
        live_count = token_counts[worker]
        valid_rows = (positions < live_count)[:, None]
        masked = jnp.where(valid_rows, cotangent[worker], jnp.zeros_like(cotangent[worker]))
        gradient = jnp.dot(features[worker].T, masked, preferred_element_type=jnp.float32) / live_count.astype(jnp.float32)
        before = params[worker]
        old_piece = lax.dynamic_index_in_dim(before.reshape(FROWS, FRAGS, KVW), fragment, 1, keepdims=False)
        drift_sum = drift_sum + live_count.astype(jnp.float32) * (global_fragment - old_piece)
        first_new = BETA_ONE * first_moment[worker] + (1.0 - BETA_ONE) * gradient
        second_new = BETA_TWO * second_moment[worker] + (1.0 - BETA_TWO) * gradient * gradient
        update = first_new / CORRECT_ONE / (jnp.sqrt(second_new / CORRECT_TWO) + ADAM_EPS)
        inner_list.append(before - LEARN_RATE * (update + DECAY_RATE * before))
        first_list.append(first_new)
        second_list.append(second_new)
    pseudo_grad = drift_sum / token_total
    momentum = NESTEROV * outer_momentum + pseudo_grad
    fresh_global = global_fragment - OUTER_RATE * (pseudo_grad + NESTEROV * momentum)
    result_list = []
    for worker in range(WORKERS):
        inner_three = inner_list[worker].reshape(FROWS, FRAGS, KVW)
        inner_piece = lax.dynamic_index_in_dim(inner_three, fragment, 1, keepdims=False)
        mixed_piece = MIXING * fresh_global + (1.0 - MIXING) * inner_piece
        merged = lax.dynamic_update_index_in_dim(inner_three, mixed_piece, fragment, 1)
        result_list.append(merged.reshape(D, KVW))
    return (jnp.stack(result_list), jnp.stack(first_list), jnp.stack(second_list), fresh_global, momentum)
```

```python
import functools

import jax
import jax.numpy as jnp
from jax import lax
from jax.experimental import pallas as pl
from jax.experimental.pallas import tpu as pltpu
from jax.sharding import PartitionSpec as P

MESH = pl.DeviceIdType.MESH
F32 = jnp.float32

FRAGS = 4
BETA_ONE = 0.9
BETA_TWO = 0.95
CORRECT_ONE = 0.6513216
CORRECT_TWO = 0.401263
ADAM_EPS = 1e-08
LEARN_RATE = 0.02
DECAY_RATE = 0.1
NESTEROV = 0.9
OUTER_RATE = 0.7
MIXING = 0.5

STRIDE = 3
GROUP = 4


def make_tree(zs, stride):
    steps = {}
    for d, length in ((1, zs // 2), (-1, zs - zs // 2 - 1)):
        stops = list(range(length, stride - 1, -stride))
        if not stops:
            stops = [length]
        for o in range(length, 0, -1):
            if o in stops:
                below = [s for s in stops if s < o]
                steps[d, o] = o - (max(below) if below else 0)
            else:
                steps[d, o] = 1
    return steps


def make_order(steps):
    kids = {}
    for (d, o), s in steps.items():
        up = (d, o - s) if o - s else (0, 0)
        kids.setdefault(up, []).append((d, o))
    half = max(o for _, o in steps)
    ready = {}

    def when(node):
        if node not in ready:
            own = 0.3 * (half - node[1])
            ready[node] = max([own] + [when(k) + 1.0 + 0.8 * steps[k] for k in kids.get(node, [])])
        return ready[node]

    order = sorted(steps, key=lambda n: (when(n), -n[1], -n[0]))
    return order, kids


def kernel(
    nw,
    zs,
    counts,
    frag_ref,
    params_h,
    first_h,
    second_h,
    glob_h,
    mom_h,
    feats_h,
    cot_h,
    new_params,
    new_first,
    new_second,
    new_glob,
    new_mom,
    feats,
    cot,
    params,
    first,
    second,
    glob,
    mom,
    term,
    crecv,
    chip,
    xrecv,
    own,
    zsend,
    zrecv,
    drift,
    wall,
    spread,
    load_sem,
    csend_sem,
    crecv_sem,
    xsend_sem,
    xrecv_sem,
    zsend_sem,
    zrecv_sem,
    wsend_sem,
    wrecv_sem,
):
    w = lax.axis_index("worker")
    k = lax.axis_index("fsdp")
    xh = k // (2 * zs)
    z = (k // 2) % zs
    c = k % 2
    rows = params.shape[0]
    tokens = feats.shape[0]
    groups = zs // GROUP

    steps = make_tree(zs, STRIDE)
    order, kids = make_order(steps)
    slot = {node: i for i, node in enumerate(steps)}
    lengths = sorted({(d, s) for (d, _), s in steps.items()})

    def at(x, zz, core):
        return (w, x * (2 * zs) + zz * 2 + core)

    core_mate = at(xh, z, 1 - c)
    x_mate = at(1 - xh, z, c)

    def z_mate(hop):
        return at(xh, (z + hop + zs) % zs, c)

    partners = [core_mate, x_mate]
    hops = sorted({h for d, s in lengths for h in (d * s, -d * s)})
    partners += [z_mate(h) for h in hops]
    partners += [((w + r) % nw, k) for r in range(1, nw)]
    barrier = pltpu.get_barrier_semaphore()
    for mate in partners:
        pl.semaphore_signal(barrier, inc=1, device_id=mate, device_id_type=MESH)

    loads = []
    for i, (src, dst) in enumerate(
        (
            (cot_h, cot),
            (feats_h, feats),
            (params_h, params),
            (glob_h, glob),
            (first_h, first),
            (second_h, second),
            (mom_h, mom),
        )
    ):
        copy = pltpu.make_async_copy(src, dst, load_sem.at[i])
        copy.start()
        loads.append(copy)

    live = counts[w]
    live_f = live.astype(F32)
    loads[0].wait()
    position = k * tokens + lax.broadcasted_iota(jnp.int32, cot.shape, 0)
    masked = jnp.where(position < live, cot[...], jnp.zeros_like(cot[...]))
    loads[1].wait()

    def group_z(i):
        p = ((i + 1) // 2) * (1 if i % 2 else -1)
        return ((z // GROUP + groups // 2 + p + groups) % groups) * GROUP

    order_of_groups = [((i + 1) // 2) * (1 if i % 2 else -1) % groups for i in range(groups)]

    def remote(src, dst, send, recv, mate):
        return pltpu.make_async_remote_copy(
            src_ref=src, dst_ref=dst, send_sem=send, recv_sem=recv, device_id=mate, device_id_type=MESH
        )

    core_copies, x_copies = [], []

    def multiply(i):
        base = group_z(i)
        for x in range(2):
            for pair in range(GROUP // 2):
                col = pl.multiple_of((x * zs + base + 2 * pair) * (2 * rows), 4 * rows)
                block = lax.dot_general(
                    feats[:, pl.ds(col, 4 * rows)],
                    masked,
                    (((0,), (0,)), ((), ())),
                    preferred_element_type=F32,
                )
                for dz in range(2):
                    for core in range(2):
                        lo = (2 * dz + core) * rows
                        term[core, x, base + 2 * pair + dz] = block[lo : lo + rows]

    def send_core(i):
        zr = pl.ds(group_z(i), GROUP)
        copy = remote(term.at[1 - c, :, zr], crecv.at[:, zr], csend_sem.at[i], crecv_sem.at[i], core_mate)
        copy.start()
        core_copies.append(copy)

    def send_x(i):
        zr = pl.ds(group_z(i), GROUP)
        core_copies[i].wait_recv()
        chip[:, zr] = term[c, :, zr] + crecv[:, zr]
        copy = remote(chip.at[1 - xh, zr], xrecv.at[zr], xsend_sem.at[i], xrecv_sem.at[i], x_mate)
        copy.start()
        x_copies.append(copy)

    multiply(0)
    pl.semaphore_wait(barrier, len(partners))
    send_core(0)
    lag = 3
    for i in range(1, groups):
        multiply(i)
        send_core(i)
        if i >= lag:
            send_x(i - lag)
    for i in range(max(groups - lag, 0), groups):
        send_x(i)

    loads[2].wait()
    loads[3].wait()
    frag = frag_ref[0]
    old = params[pl.ds(0, rows // FRAGS, stride=FRAGS), :]
    for f in range(1, FRAGS):
        old = jnp.where(frag == f, params[pl.ds(f, rows // FRAGS, stride=FRAGS), :], old)
    mine = live_f * (glob[...] - old)
    drift[...] = mine
    wall[w] = mine
    worker_copies = []
    for r in range(1, nw):
        copy = remote(drift, wall.at[w], wsend_sem.at[r], wrecv_sem.at[w], ((w + r) % nw, k))
        copy.start()
        worker_copies.append(copy)

    def outer():
        for r in range(1, nw):
            sender = (w + r) % nw
            remote(drift, wall.at[sender], wsend_sem.at[r], wrecv_sem.at[sender], (sender, k)).wait_recv()
        total = wall[0]
        token_total = counts[0]
        for i in range(1, nw):
            total = total + wall[i]
            token_total = token_total + counts[i]
        pseudo = total / token_total.astype(F32)
        loads[6].wait()
        momentum = NESTEROV * mom[...] + pseudo
        fresh = glob[...] - OUTER_RATE * (pseudo + NESTEROV * momentum)
        new_mom[...] = momentum
        new_glob[...] = fresh
        for f in range(FRAGS):
            spread[pl.ds(f, rows // FRAGS, stride=FRAGS), :] = fresh
        loads[4].wait()
        loads[5].wait()

    done = set()

    def need(d, o):
        rel = {((r + d * o) // GROUP) % groups for r in range(GROUP)}
        for i in range(groups):
            where = (groups // 2 + order_of_groups[i]) % groups
            if where in rel and i not in done:
                done.add(i)
                x_copies[i].wait_recv()
                zr = pl.ds(group_z(i), GROUP)
                own[zr] = chip[xh, zr] + xrecv[zr]

    z_copies = {}

    def gather(node, zz):
        total = own[zz]
        for kid in kids.get(node, []):
            z_copies[kid].wait_recv()
            total = total + zrecv[slot[kid]]
        return total

    for count, node in enumerate(order):
        d, o = node
        need(d, o)
        zz = (z + d * o + zs) % zs
        i = slot[node]
        if kids.get(node):
            zsend[i] = gather(node, zz)
            src = zsend.at[i]
        else:
            src = own.at[zz]
        copy = remote(src, zrecv.at[i], zsend_sem.at[i], zrecv_sem.at[i], z_mate(d * steps[node]))
        copy.start()
        z_copies[node] = copy
        if count == (3 * len(order)) // 4:
            outer()

    need(1, 0)
    gradient = gather((0, 0), z) / live_f
    first_new = BETA_ONE * first[...] + (1.0 - BETA_ONE) * gradient
    second_new = BETA_TWO * second[...] + (1.0 - BETA_TWO) * gradient * gradient
    update = first_new / CORRECT_ONE / (jnp.sqrt(second_new / CORRECT_TWO) + ADAM_EPS)
    before = params[...]
    inner = before - LEARN_RATE * (update + DECAY_RATE * before)
    chosen = lax.broadcasted_iota(jnp.int32, inner.shape, 0) % FRAGS == frag
    new_params[...] = jnp.where(chosen, MIXING * spread[...] + (1.0 - MIXING) * inner, inner)
    new_first[...] = first_new
    new_second[...] = second_new

    for copy in core_copies + x_copies + worker_copies + list(z_copies.values()):
        copy.wait_send()


def solution(mesh):
    nw = mesh.shape["worker"]
    zs = mesh.shape["fsdp"] // 4

    def step(params, first, second, glob, mom, features, cotangent, counts, frag):
        rows, width = params.shape[1:]
        frows = glob.shape[0]
        tokens, depth = features.shape[1:]
        vm = pltpu.VMEM
        dma = pltpu.SemaphoreType.DMA
        messages = zs - 1
        groups = zs // GROUP
        tile = (rows, width)
        big = jax.ShapeDtypeStruct(tile, F32)
        small = jax.ShapeDtypeStruct((frows, width), F32)
        smem = pl.BlockSpec(memory_space=pltpu.SMEM)
        hbm = pl.BlockSpec(memory_space=pl.ANY)
        out = pl.pallas_call(
            functools.partial(kernel, nw, zs),
            out_shape=(big, big, big, small, small),
            in_specs=[smem, smem] + [hbm] * 7,
            out_specs=[pl.BlockSpec(memory_space=vm)] * 5,
            scratch_shapes=[
                vm((tokens, depth), jnp.bfloat16),
                vm((tokens, width), jnp.bfloat16),
                vm(tile, F32),
                vm(tile, F32),
                vm(tile, F32),
                vm((frows, width), F32),
                vm((frows, width), F32),
                vm((2, 2, zs) + tile, F32),
                vm((2, zs) + tile, F32),
                vm((2, zs) + tile, F32),
                vm((zs,) + tile, F32),
                vm((zs,) + tile, F32),
                vm((messages,) + tile, F32),
                vm((messages,) + tile, F32),
                vm((frows, width), F32),
                vm((nw, frows, width), F32),
                vm(tile, F32),
                dma((7,)),
                dma((groups,)),
                dma((groups,)),
                dma((groups,)),
                dma((groups,)),
                dma((messages,)),
                dma((messages,)),
                dma((nw,)),
                dma((nw,)),
            ],
            compiler_params=pltpu.CompilerParams(collective_id=0, has_side_effects=True),
            name="diloco_step",
        )(counts, frag, params[0], first[0], second[0], glob, mom, features[0], cotangent[0])
        return (out[0][None], out[1][None], out[2][None], out[3], out[4])

    held = P("worker", "fsdp", None)
    shared = P("fsdp", None)
    return jax.shard_map(
        step,
        mesh=mesh,
        in_specs=(held, held, held, shared, shared, held, held, P(), P()),
        out_specs=(held, held, held, shared, shared),
        check_vma=False,
    )
```

```python
import functools

import jax
import jax.numpy as jnp
from jax import lax
from jax.experimental import pallas as pl
from jax.experimental.pallas import tpu as pltpu
from jax.sharding import PartitionSpec as P

MESH = pl.DeviceIdType.MESH
F32 = jnp.float32

FRAGS = 4
BETA_ONE = 0.9
BETA_TWO = 0.95
CORRECT_ONE = 0.6513216
CORRECT_TWO = 0.401263
ADAM_EPS = 1e-08
LEARN_RATE = 0.02
DECAY_RATE = 0.1
NESTEROV = 0.9
OUTER_RATE = 0.7
MIXING = 0.5

VMEM_LIMIT = 16 * 1024 * 1024
GROUP = 2
STOPS = {1: (13, 11, 7, 4), -1: (11, 7, 4)}

HOP, WIRE, STOP, FIRST, NEXT = 0.78, 0.35, 0.88, 4.8, 0.71


def make_tree(zs):
    steps = {}
    for d, length in ((1, zs // 2), (-1, zs - zs // 2 - 1)):
        stops = [0] + [s for s in STOPS[d] if s <= length]
        for o in range(1, length + 1):
            if o in stops:
                steps[d, o] = o - max(s for s in stops if s < o)
            else:
                steps[d, o] = o - min(stops, key=lambda s: (abs(s - o), s))
    return steps


def turn(i, groups):
    return (groups // 2 + ((i + 1) // 2) * (1 if i % 2 else -1)) % groups


def groups_of(d, o, groups):
    return {((r + d * o) // GROUP) % groups for r in range(GROUP)}


def make_order(steps, zs):
    groups = zs // GROUP
    arrival = {turn(i, groups): FIRST + NEXT * i for i in range(groups)}
    kids = {}
    for (d, o), s in steps.items():
        kids.setdefault((d, o - s) if o - s else (0, 0), []).append((d, o))
    ready = {}
    left = {n: len(kids.get(n, [])) for n in steps}
    at = {n: max(arrival[g] for g in groups_of(*n, groups)) for n in steps}
    events = [(at[n], n, 0) for n in steps if not left[n]]
    free = {1: 0.0, -1: 0.0}
    while events:
        events.sort()
        t, n, hop = events.pop(0)
        step = steps[n]
        if hop == 0:
            ready[n] = t
        if hop < abs(step):
            link = n[0] if step > 0 else -n[0]
            begin = max(t, free[link])
            free[link] = begin + WIRE
            last = hop + 1 == abs(step)
            events.append((begin + HOP + (WIRE + STOP if last else 0.0), n, hop + 1))
            continue
        up = (n[0], n[1] - step)
        if up[1]:
            left[up] -= 1
            at[up] = max(at[up], t)
            if not left[up]:
                events.append((at[up], up, 0))
    return sorted(steps, key=lambda n: (ready[n], -n[1], -n[0])), kids


def kernel(
    nw,
    zs,
    counts_h,
    frag_ref,
    params_h,
    first_h,
    second_h,
    glob_h,
    mom_h,
    feats_h,
    cot_h,
    result,
    counts,
    feats,
    cot,
    params,
    first,
    second,
    glob,
    mom,
    term,
    crecv,
    chip,
    xrecv,
    own,
    zsend,
    zrecv,
    drift,
    wall,
    spread,
    load_sem,
    csend_sem,
    crecv_sem,
    xsend_sem,
    xrecv_sem,
    zsend_sem,
    zrecv_sem,
    wsend_sem,
    wrecv_sem,
):
    w = lax.axis_index("worker")
    k = lax.axis_index("fsdp")
    xh = k // (2 * zs)
    z = (k // 2) % zs
    c = k % 2
    rows = params.shape[0]
    tokens = feats.shape[0]
    groups = zs // GROUP

    steps = make_tree(zs)
    order, kids = make_order(steps, zs)
    slot = {node: i for i, node in enumerate(steps)}
    lengths = sorted({(d, s) for (d, _), s in steps.items()})

    def at(x, zz, core):
        return (w, x * (2 * zs) + zz * 2 + core)

    core_mate = at(xh, z, 1 - c)
    x_mate = at(1 - xh, z, c)

    def z_mate(hop):
        return at(xh, (z + hop + zs) % zs, c)

    partners = [core_mate, x_mate]
    hops = sorted({h for d, s in lengths for h in (d * s, -d * s)})
    partners += [z_mate(h) for h in hops]
    partners += [((w + r) % nw, k) for r in range(1, nw)]
    barrier = pltpu.get_barrier_semaphore()
    for mate in partners:
        pl.semaphore_signal(barrier, inc=1, device_id=mate, device_id_type=MESH)

    loads = []
    for i, (src, dst) in enumerate(
        (
            (cot_h, cot),
            (feats_h, feats),
            (params_h, params),
            (glob_h, glob),
            (first_h, first),
            (second_h, second),
            (mom_h, mom),
            (counts_h, counts),
        )
    ):
        copy = pltpu.make_async_copy(src, dst, load_sem.at[i])
        copy.start()
        loads.append(copy)

    loads[7].wait()
    live = counts[w]
    live_f = live.astype(F32)
    loads[0].wait()
    position = k * tokens + lax.broadcasted_iota(jnp.int32, cot.shape, 0)
    masked = jnp.where(position < live, cot[...], jnp.zeros_like(cot[...]))
    loads[1].wait()

    def group_z(i):
        return ((z // GROUP + turn(i, groups)) % groups) * GROUP

    def remote(src, dst, send, recv, mate):
        return pltpu.make_async_remote_copy(
            src_ref=src, dst_ref=dst, send_sem=send, recv_sem=recv, device_id=mate, device_id_type=MESH
        )

    core_copies, x_copies = [], []

    def multiply(i):
        base = group_z(i)
        for x in range(2):
            for pair in range(GROUP // 2):
                col = pl.multiple_of((x * zs + base + 2 * pair) * (2 * rows), 4 * rows)
                block = lax.dot_general(
                    feats[:, pl.ds(col, 4 * rows)],
                    masked,
                    (((0,), (0,)), ((), ())),
                    preferred_element_type=F32,
                )
                for dz in range(2):
                    for core in range(2):
                        lo = (2 * dz + core) * rows
                        term[core, x, base + 2 * pair + dz] = block[lo : lo + rows]

    def send_core(i):
        zr = pl.ds(group_z(i), GROUP)
        copy = remote(term.at[1 - c, :, zr], crecv.at[:, zr], csend_sem.at[i], crecv_sem.at[i], core_mate)
        copy.start()
        core_copies.append(copy)

    def send_x(i):
        zr = pl.ds(group_z(i), GROUP)
        core_copies[i].wait_recv()
        chip[:, zr] = term[c, :, zr] + crecv[:, zr]
        copy = remote(chip.at[1 - xh, zr], xrecv.at[zr], xsend_sem.at[i], xrecv_sem.at[i], x_mate)
        copy.start()
        x_copies.append(copy)

    for i in range(groups):
        multiply(i)

    loads[2].wait()
    loads[3].wait()
    frag = frag_ref[0]
    old = params[pl.ds(0, rows // FRAGS, stride=FRAGS), :]
    for f in range(1, FRAGS):
        old = jnp.where(frag == f, params[pl.ds(f, rows // FRAGS, stride=FRAGS), :], old)
    mine = live_f * (glob[...] - old)
    drift[...] = mine
    wall[w] = mine

    pl.semaphore_wait(barrier, len(partners))
    for i in range(groups):
        send_core(i)
    for i in range(groups):
        send_x(i)
    worker_copies = []
    for r in range(1, nw):
        copy = remote(drift, wall.at[w], wsend_sem.at[r], wrecv_sem.at[w], ((w + r) % nw, k))
        copy.start()
        worker_copies.append(copy)

    def outer():
        for r in range(1, nw):
            sender = (w + r) % nw
            remote(drift, wall.at[sender], wsend_sem.at[r], wrecv_sem.at[sender], (sender, k)).wait_recv()
        total = wall[0]
        token_total = counts[0]
        for i in range(1, nw):
            total = total + wall[i]
            token_total = token_total + counts[i]
        pseudo = total / token_total.astype(F32)
        loads[6].wait()
        momentum = NESTEROV * mom[...] + pseudo
        fresh = glob[...] - OUTER_RATE * (pseudo + NESTEROV * momentum)
        result[pl.ds(3 * rows + fresh.shape[0], fresh.shape[0]), :] = momentum
        result[pl.ds(3 * rows, fresh.shape[0]), :] = fresh
        for f in range(FRAGS):
            spread[pl.ds(f, rows // FRAGS, stride=FRAGS), :] = fresh
        loads[4].wait()
        loads[5].wait()

    done = set()

    def need(d, o):
        where = groups_of(d, o, groups)
        for i in range(groups):
            if turn(i, groups) in where and i not in done:
                done.add(i)
                x_copies[i].wait_recv()
                zr = pl.ds(group_z(i), GROUP)
                own[zr] = chip[xh, zr] + xrecv[zr]

    z_copies = {}

    def gather(node, zz):
        total = own[zz]
        for kid in kids.get(node, []):
            z_copies[kid].wait_recv()
            total = total + zrecv[slot[kid]]
        return total

    for count, node in enumerate(order):
        d, o = node
        need(d, o)
        zz = (z + d * o + zs) % zs
        i = slot[node]
        if kids.get(node):
            zsend[i] = gather(node, zz)
            src = zsend.at[i]
        else:
            src = own.at[zz]
        copy = remote(src, zrecv.at[i], zsend_sem.at[i], zrecv_sem.at[i], z_mate(d * steps[node]))
        copy.start()
        z_copies[node] = copy
        if count == (2 * len(order)) // 3:
            outer()

    need(1, 0)
    gradient = gather((0, 0), z) / live_f
    first_new = BETA_ONE * first[...] + (1.0 - BETA_ONE) * gradient
    second_new = BETA_TWO * second[...] + (1.0 - BETA_TWO) * gradient * gradient
    update = first_new / CORRECT_ONE / (jnp.sqrt(second_new / CORRECT_TWO) + ADAM_EPS)
    before = params[...]
    inner = before - LEARN_RATE * (update + DECAY_RATE * before)
    chosen = lax.broadcasted_iota(jnp.int32, inner.shape, 0) % FRAGS == frag
    result[pl.ds(0, rows), :] = jnp.where(chosen, MIXING * spread[...] + (1.0 - MIXING) * inner, inner)
    result[pl.ds(rows, rows), :] = first_new
    result[pl.ds(2 * rows, rows), :] = second_new

    for copy in core_copies + x_copies + worker_copies + list(z_copies.values()):
        copy.wait_send()


def hand_out(packed, *refs):
    outs, sems = refs[:-1], refs[-1]
    copies, lo = [], 0
    for i, out in enumerate(outs):
        n = out.shape[0]
        copy = pltpu.make_async_copy(packed.at[pl.ds(lo, n)], out, sems.at[i])
        copy.start()
        copies.append(copy)
        lo += n
    for copy in copies:
        copy.wait()


def solution(mesh):
    nw = mesh.shape["worker"]
    zs = mesh.shape["fsdp"] // 4

    def step(params, first, second, glob, mom, features, cotangent, counts, frag):
        rows, width = params.shape[1:]
        frows = glob.shape[0]
        tokens, depth = features.shape[1:]
        vm = pltpu.VMEM
        dma = pltpu.SemaphoreType.DMA
        messages = zs - 1
        groups = zs // GROUP
        tile = (rows, width)
        in_hbm = functools.partial(pltpu.with_memory_space_constraint, memory_space=pltpu.HBM)
        big = jax.ShapeDtypeStruct(tile, F32)
        small = jax.ShapeDtypeStruct((frows, width), F32)
        hbm = pl.BlockSpec(memory_space=pl.ANY)
        packed = pl.pallas_call(
            functools.partial(kernel, nw, zs),
            out_shape=jax.ShapeDtypeStruct((3 * rows + 2 * frows, width), F32),
            in_specs=[hbm, pl.BlockSpec(memory_space=pltpu.SMEM)] + [hbm] * 7,
            out_specs=pl.BlockSpec(memory_space=vm),
            scratch_shapes=[
                pltpu.SMEM((nw,), jnp.int32),
                vm((tokens, depth), jnp.bfloat16),
                vm((tokens, width), jnp.bfloat16),
                vm(tile, F32),
                vm(tile, F32),
                vm(tile, F32),
                vm((frows, width), F32),
                vm((frows, width), F32),
                vm((2, 2, zs) + tile, F32),
                vm((2, zs) + tile, F32),
                vm((2, zs) + tile, F32),
                vm((zs,) + tile, F32),
                vm((zs,) + tile, F32),
                vm((messages,) + tile, F32),
                vm((messages,) + tile, F32),
                vm((frows, width), F32),
                vm((nw, frows, width), F32),
                vm(tile, F32),
                dma((8,)),
                dma((groups,)),
                dma((groups,)),
                dma((groups,)),
                dma((groups,)),
                dma((messages,)),
                dma((messages,)),
                dma((nw,)),
                dma((nw,)),
            ],
            compiler_params=pltpu.CompilerParams(collective_id=0, has_side_effects=True, vmem_limit_bytes=VMEM_LIMIT),
            name="diloco_step",
        )(in_hbm(counts), frag, *map(in_hbm, (params[0], first[0], second[0], glob, mom, features[0], cotangent[0])))
        out = pl.pallas_call(
            hand_out,
            out_shape=(big, big, big, small, small),
            in_specs=[hbm],
            out_specs=[hbm] * 5,
            scratch_shapes=[dma((5,))],
            compiler_params=pltpu.CompilerParams(vmem_limit_bytes=1024 * 1024),
            name="hand_out",
        )(packed)
        return (out[0][None], out[1][None], out[2][None], out[3], out[4])

    held = P("worker", "fsdp", None)
    shared = P("fsdp", None)
    return jax.shard_map(
        step,
        mesh=mesh,
        in_specs=(held, held, held, shared, shared, held, held, P(), P()),
        out_specs=(held, held, held, shared, shared),
        check_vma=False,
    )
```

```python
import functools

import jax
import jax.numpy as jnp
from jax import lax
from jax.experimental import pallas as pl
from jax.experimental.pallas import tpu as pltpu
from jax.sharding import PartitionSpec as P

MESH = pl.DeviceIdType.MESH
F32 = jnp.float32

FRAGS = 4
BETA_ONE = 0.9
BETA_TWO = 0.95
CORRECT_ONE = 0.6513216
CORRECT_TWO = 0.401263
ADAM_EPS = 1e-08
LEARN_RATE = 0.02
DECAY_RATE = 0.1
NESTEROV = 0.9
OUTER_RATE = 0.7
MIXING = 0.5

VMEM_LIMIT = 16 * 1024 * 1024
GROUP = 2
CORE_PARTS = (0, 1, 2, 4, 8, 16)
X_PARTS = tuple(range(15)) + (16, 18, 20, 22, 24, 28, 32)
STOPS = {1: (13, 11, 7, 3), -1: (13, 11, 7, 3)}
NEAR = 2

HOP, WIRE, STOP, FIRST, NEXT, SLACK = 0.78, 0.35, 0.88, 3.9, 0.36, 0.8


def make_tree(zs):
    steps = {}
    for d, length in ((1, zs // 2), (-1, zs - zs // 2 - 1)):
        stops = [0] + [s for s in STOPS[d] if s <= length]
        for o in range(1, length + 1):
            if o in stops:
                steps[d, o] = o - max(s for s in stops if s < o)
            else:
                steps[d, o] = o - min(stops, key=lambda s: (abs(s - o), s))
    return steps


def turn(i, groups):
    return (groups // 2 + ((i + 1) // 2) * (1 if i % 2 else -1)) % groups


def part_of(bounds, i):
    return max(p for p, first in enumerate(bounds) if first <= i)


def groups_of(d, o, groups):
    return {((r + d * o) // GROUP) % groups for r in range(GROUP)}


def far_first(steps):
    return sorted(list(steps) + [(0, 0)], key=lambda n: (-n[1], -n[0]))


def make_order(steps, zs):
    arrival = {n: FIRST + NEXT * i for i, n in enumerate(far_first(steps))}
    kids = {}
    for (d, o), s in steps.items():
        kids.setdefault((d, o - s) if o - s else (0, 0), []).append((d, o))
    ready = {}
    left = {n: len(kids.get(n, [])) for n in steps}
    at = {n: arrival[n] for n in steps}
    events = [(at[n], n, 0) for n in steps if not left[n]]
    free = {1: 0.0, -1: 0.0}
    while events:
        events.sort()
        t, n, hop = events.pop(0)
        step = steps[n]
        if hop == 0:
            ready[n] = t + (SLACK if n in kids else 0.0)
        if hop < abs(step):
            link = n[0] if step > 0 else -n[0]
            begin = max(t, free[link])
            free[link] = begin + WIRE
            last = hop + 1 == abs(step)
            events.append((begin + HOP + (WIRE + STOP if last else 0.0), n, hop + 1))
            continue
        up = (n[0], n[1] - step)
        if up[1]:
            left[up] -= 1
            at[up] = max(at[up], t)
            if not left[up]:
                events.append((at[up], up, 0))
    return sorted(steps, key=lambda n: (ready[n], -n[1], -n[0])), kids


def kernel(
    nw,
    zs,
    counts_h,
    frag_ref,
    params_h,
    first_h,
    second_h,
    glob_h,
    mom_h,
    feats_h,
    cot_h,
    result,
    counts,
    feats,
    cot,
    params,
    first,
    second,
    glob,
    mom,
    term,
    crecv,
    chip,
    xrecv,
    own,
    zsend,
    zrecv,
    drift,
    wall,
    spread,
    load_sem,
    csend_sem,
    crecv_sem,
    xsend_sem,
    xrecv_sem,
    zsend_sem,
    zrecv_sem,
    wsend_sem,
    wrecv_sem,
    far_sem,
):
    w = lax.axis_index("worker")
    k = lax.axis_index("fsdp")
    xh = k // (2 * zs)
    z = (k // 2) % zs
    c = k % 2
    rows = params.shape[0]
    tokens = feats.shape[0]
    groups = zs // GROUP

    steps = make_tree(zs)
    order, kids = make_order(steps, zs)
    slot = {}
    for kin in kids.values():
        for node in kin:
            slot[node] = len(slot)
    channel = {up: i for i, up in enumerate(kids)}
    def at(x, zz, core):
        return (w, x * (2 * zs) + zz * 2 + core)

    core_mate = at(xh, z, 1 - c)
    x_mate = at(1 - xh, z, c)

    def z_mate(hop):
        return at(xh, (z + hop + zs) % zs, c)

    y, xl, ny = w // 2, w % 2, nw // 2
    side_mate = (2 * y + 1 - xl, k)
    up_mate, down_mate = (2 * ((y + 1) % ny) + xl, k), (2 * ((y + ny - 1) % ny) + xl, k)
    partners = [core_mate, x_mate] + [z_mate(h) for h in (1, -1, NEAR, -NEAR)]
    if nw > 1:
        partners.append(side_mate)
    if ny > 1:
        partners += [up_mate, down_mate]
    barrier = pltpu.get_barrier_semaphore()
    for mate in partners:
        pl.semaphore_signal(barrier, inc=1, device_id=mate, device_id_type=MESH)

    loads = []
    for i, (src, dst) in enumerate(
        (
            (cot_h, cot),
            (feats_h, feats),
            (params_h, params),
            (glob_h, glob),
            (first_h, first),
            (second_h, second),
            (mom_h, mom),
            (counts_h, counts),
        )
    ):
        copy = pltpu.make_async_copy(src, dst, load_sem.at[i])
        copy.start()
        loads.append(copy)

    loads[7].wait()
    live = counts[w]
    live_f = live.astype(F32)
    loads[0].wait()
    position = k * tokens + lax.broadcasted_iota(jnp.int32, cot.shape, 0)
    masked = jnp.where(position < live, cot[...], jnp.zeros_like(cot[...]))
    loads[1].wait()

    def group_z(i):
        return ((z // GROUP + turn(i, groups)) % groups) * GROUP

    def remote(src, dst, send, recv, mate):
        return pltpu.make_async_remote_copy(
            src_ref=src, dst_ref=dst, send_sem=send, recv_sem=recv, device_id=mate, device_id_type=MESH
        )

    core_done, reduced = set(), set()

    def multiply(i):
        base = group_z(i)
        for x in range(2):
            for pair in range(GROUP // 2):
                col = pl.multiple_of((x * zs + base + 2 * pair) * (2 * rows), 4 * rows)
                block = lax.dot_general(
                    feats[:, pl.ds(col, 4 * rows)],
                    masked,
                    (((0,), (0,)), ((), ())),
                    preferred_element_type=F32,
                )
                for dz in range(2):
                    for core in range(2):
                        lo = (2 * dz + core) * rows
                        term[core, x, base + 2 * pair + dz] = block[lo : lo + rows]

    def send_core(i):
        zr = pl.ds(group_z(i), GROUP)
        copy = remote(term.at[1 - c, :, zr], crecv.at[:, zr], csend_sem, crecv_sem.at[part_of(CORE_PARTS, i)], core_mate)
        copy.start()

    far = far_first(steps)

    def z_of(node):
        return (z + node[0] * node[1] + zs) % zs

    def reduce_pair(i):
        part = part_of(CORE_PARTS, i)
        if part not in core_done:
            core_done.add(part)
            wait_core(part)
        zr = pl.ds(group_z(i), GROUP)
        chip[:, zr] = term[c, :, zr] + crecv[:, zr]

    def send_x(i):
        where = groups_of(*far[i], groups)
        for j in range(groups):
            if turn(j, groups) in where and j not in reduced:
                reduced.add(j)
                reduce_pair(j)
        zz = z_of(far[i])
        remote(chip.at[1 - xh, zz], xrecv.at[zz], xsend_sem, xrecv_sem.at[part_of(X_PARTS, i)], x_mate).start()

    def wait_core(part):
        n = GROUP * (CORE_PARTS[part + 1] - CORE_PARTS[part])
        zr = pl.ds(0, n)
        remote(term.at[1 - c, :, zr], crecv.at[:, zr], csend_sem, crecv_sem.at[part], core_mate).wait_recv()

    def wait_x(part):
        zr = pl.ds(0, X_PARTS[part + 1] - X_PARTS[part])
        remote(chip.at[1 - xh, zr], xrecv.at[zr], xsend_sem, xrecv_sem.at[part], x_mate).wait_recv()

    for i in range(groups):
        multiply(i)

    loads[2].wait()
    loads[3].wait()
    frag = frag_ref[0]
    old = params[pl.ds(0, rows // FRAGS, stride=FRAGS), :]
    for f in range(1, FRAGS):
        old = jnp.where(frag == f, params[pl.ds(f, rows // FRAGS, stride=FRAGS), :], old)
    mine = live_f * (glob[...] - old)
    drift[...] = mine
    wall[w] = mine

    pl.semaphore_wait(barrier, len(partners))
    for i in range(groups):
        send_core(i)
    for h in (NEAR, -NEAR):
        pl.semaphore_signal(far_sem, inc=1, device_id=z_mate(h), device_id_type=MESH)
    if nw > 1:
        remote(drift, wall.at[w], wsend_sem.at[0], wrecv_sem.at[0], side_mate).start()
    for i in range(zs):
        send_x(i)

    def block(i):
        return wall.at[pl.ds(2 * ((y + i + ny) % ny), 2)]

    def worker_pairs():
        if nw > 1:
            remote(drift, drift, wsend_sem.at[0], wrecv_sem.at[0], side_mate).wait_recv()
        if ny > 1:
            remote(block(0), block(0), wsend_sem.at[1], wrecv_sem.at[1], up_mate).start()
            remote(block(0), block(0), wsend_sem.at[2], wrecv_sem.at[2], down_mate).start()

    def worker_relay():
        if ny > 1:
            remote(block(-1), block(-1), wsend_sem.at[0], wrecv_sem.at[1], up_mate).wait_recv()
            remote(block(-1), block(-1), wsend_sem.at[3], wrecv_sem.at[3], up_mate).start()

    def outer():
        if ny > 1:
            remote(block(1), block(1), wsend_sem.at[0], wrecv_sem.at[2], down_mate).wait_recv()
            remote(block(2), block(2), wsend_sem.at[0], wrecv_sem.at[3], up_mate).wait_recv()
        total = wall[0]
        token_total = counts[0]
        for i in range(1, nw):
            total = total + wall[i]
            token_total = token_total + counts[i]
        pseudo = total / token_total.astype(F32)
        loads[6].wait()
        momentum = NESTEROV * mom[...] + pseudo
        fresh = glob[...] - OUTER_RATE * (pseudo + NESTEROV * momentum)
        result[pl.ds(3 * rows + fresh.shape[0], fresh.shape[0]), :] = momentum
        result[pl.ds(3 * rows, fresh.shape[0]), :] = fresh
        for f in range(FRAGS):
            spread[pl.ds(f, rows // FRAGS, stride=FRAGS), :] = fresh
        loads[4].wait()
        loads[5].wait()

    done = set()

    def need(node):
        part = part_of(X_PARTS, far.index(node))
        if part not in done:
            done.add(part)
            wait_x(part)
            for other in far[X_PARTS[part] : X_PARTS[part + 1]]:
                zz = z_of(other)
                own[zz] = chip[xh, zz] + xrecv[zz]

    def gather(node, zz):
        kin = kids[node]
        lo = slot[kin[0]]
        zr = pl.ds(lo, len(kin))
        remote(zrecv.at[zr], zrecv.at[zr], zsend_sem, zrecv_sem.at[channel[node]], x_mate).wait_recv()
        total = own[zz]
        for i in range(lo, lo + len(kin)):
            total = total + zrecv[i]
        return total

    pl.semaphore_wait(far_sem, 2)
    for count, node in enumerate(order):
        d, o = node
        need(node)
        zz = z_of(node)
        i = slot[node]
        if kids.get(node):
            zsend[i] = gather(node, zz)
            src = zsend.at[i]
        else:
            src = own.at[zz]
        up = (d, o - steps[node]) if o - steps[node] else (0, 0)
        remote(src, zrecv.at[i], zsend_sem, zrecv_sem.at[channel[up]], z_mate(d * steps[node])).start()
        if count == len(order) // 3:
            worker_pairs()
        if count == len(order) // 2:
            worker_relay()
        if count == (3 * len(order)) // 4:
            outer()

    need((0, 0))
    gradient = gather((0, 0), z) / live_f
    first_new = BETA_ONE * first[...] + (1.0 - BETA_ONE) * gradient
    second_new = BETA_TWO * second[...] + (1.0 - BETA_TWO) * gradient * gradient
    update = first_new / CORRECT_ONE / (jnp.sqrt(second_new / CORRECT_TWO) + ADAM_EPS)
    before = params[...]
    inner = before - LEARN_RATE * (update + DECAY_RATE * before)
    chosen = lax.broadcasted_iota(jnp.int32, inner.shape, 0) % FRAGS == frag
    result[pl.ds(0, rows), :] = jnp.where(chosen, MIXING * spread[...] + (1.0 - MIXING) * inner, inner)
    result[pl.ds(rows, rows), :] = first_new
    result[pl.ds(2 * rows, rows), :] = second_new

    remote(crecv, crecv, csend_sem, crecv_sem.at[0], core_mate).wait_send()
    remote(xrecv, xrecv, xsend_sem, xrecv_sem.at[0], x_mate).wait_send()
    remote(zrecv, zrecv, zsend_sem, zrecv_sem.at[0], x_mate).wait_send()
    if nw > 1:
        remote(drift, drift, wsend_sem.at[0], wrecv_sem.at[0], side_mate).wait_send()
    for i in range(1, 4 if ny > 1 else 0):
        remote(block(0), block(0), wsend_sem.at[i], wrecv_sem.at[i], up_mate).wait_send()


def hand_out(packed, *refs):
    outs, sems = refs[:-1], refs[-1]
    copies, lo = [], 0
    for i, out in enumerate(outs):
        n = out.shape[0]
        copy = pltpu.make_async_copy(packed.at[pl.ds(lo, n)], out, sems.at[i])
        copy.start()
        copies.append(copy)
        lo += n
    for copy in copies:
        copy.wait()


def solution(mesh):
    nw = mesh.shape["worker"]
    zs = mesh.shape["fsdp"] // 4

    def step(params, first, second, glob, mom, features, cotangent, counts, frag):
        rows, width = params.shape[1:]
        frows = glob.shape[0]
        tokens, depth = features.shape[1:]
        vm = pltpu.VMEM
        dma = pltpu.SemaphoreType.DMA
        messages = zs - 1
        stops = len(make_order(make_tree(zs), zs)[1])
        groups = zs // GROUP
        tile = (rows, width)
        in_hbm = functools.partial(pltpu.with_memory_space_constraint, memory_space=pltpu.HBM)
        big = jax.ShapeDtypeStruct(tile, F32)
        small = jax.ShapeDtypeStruct((frows, width), F32)
        hbm = pl.BlockSpec(memory_space=pl.ANY)
        packed = pl.pallas_call(
            functools.partial(kernel, nw, zs),
            out_shape=jax.ShapeDtypeStruct((3 * rows + 2 * frows, width), F32),
            in_specs=[hbm, pl.BlockSpec(memory_space=pltpu.SMEM)] + [hbm] * 7,
            out_specs=pl.BlockSpec(memory_space=vm),
            scratch_shapes=[
                pltpu.SMEM((nw,), jnp.int32),
                vm((tokens, depth), jnp.bfloat16),
                vm((tokens, width), jnp.bfloat16),
                vm(tile, F32),
                vm(tile, F32),
                vm(tile, F32),
                vm((frows, width), F32),
                vm((frows, width), F32),
                vm((2, 2, zs) + tile, F32),
                vm((2, zs) + tile, F32),
                vm((2, zs) + tile, F32),
                vm((zs,) + tile, F32),
                vm((zs,) + tile, F32),
                vm((messages,) + tile, F32),
                vm((messages,) + tile, F32),
                vm((frows, width), F32),
                vm((nw, frows, width), F32),
                vm(tile, F32),
                dma((8,)),
                dma(()),
                dma((len(CORE_PARTS) - 1,)),
                dma(()),
                dma((len(X_PARTS) - 1,)),
                dma(()),
                dma((stops,)),
                dma((4,)),
                dma((4,)),
                pltpu.SemaphoreType.REGULAR,
            ],
            compiler_params=pltpu.CompilerParams(collective_id=0, has_side_effects=True, vmem_limit_bytes=VMEM_LIMIT),
            name="diloco_step",
        )(in_hbm(counts), frag, *map(in_hbm, (params[0], first[0], second[0], glob, mom, features[0], cotangent[0])))
        out = pl.pallas_call(
            hand_out,
            out_shape=(big, big, big, small, small),
            in_specs=[hbm],
            out_specs=[hbm] * 5,
            scratch_shapes=[dma((5,))],
            compiler_params=pltpu.CompilerParams(vmem_limit_bytes=1024 * 1024),
            name="hand_out",
        )(packed)
        return (out[0][None], out[1][None], out[2][None], out[3], out[4])

    held = P("worker", "fsdp", None)
    shared = P("fsdp", None)
    return jax.shard_map(
        step,
        mesh=mesh,
        in_specs=(held, held, held, shared, shared, held, held, P(), P()),
        out_specs=(held, held, held, shared, shared),
        check_vma=False,
    )
```

```python
import functools

import jax
import jax.numpy as jnp
from jax import lax
from jax.experimental import pallas as pl
from jax.experimental.pallas import tpu as pltpu
from jax.sharding import PartitionSpec as P

MESH = pl.DeviceIdType.MESH
F32 = jnp.float32

FRAGS = 4
BETA_ONE = 0.9
BETA_TWO = 0.95
CORRECT_ONE = 0.6513216
CORRECT_TWO = 0.401263
ADAM_EPS = 1e-08
LEARN_RATE = 0.02
DECAY_RATE = 0.1
NESTEROV = 0.9
OUTER_RATE = 0.7
MIXING = 0.5

VMEM_LIMIT = 16 * 1024 * 1024
GROUP = 2
CORE_PARTS = (0, 1, 2, 4, 8, 16)
X_PARTS = tuple(range(9)) + (10, 12, 14, 16, 18, 20, 24, 28, 32)
STOPS = {1: (12, 8, 4), -1: (12, 8, 4)}
NEAR = 2

HOP, WIRE, STOP, FIRST, NEXT, SLACK = 0.78, 0.35, 0.88, 5.0, 0.36, -1.5


def make_tree(zs):
    steps = {}
    for d, length in ((1, zs // 2), (-1, zs - zs // 2 - 1)):
        stops = [0] + [s for s in STOPS[d] if s <= length]
        for o in range(1, length + 1):
            if o in stops:
                steps[d, o] = o - max(s for s in stops if s < o)
            else:
                steps[d, o] = o - min(stops, key=lambda s: (abs(s - o), s))
    return steps


def turn(i, groups):
    return (groups // 2 + ((i + 1) // 2) * (1 if i % 2 else -1)) % groups


def part_of(bounds, i):
    return max(p for p, first in enumerate(bounds) if first <= i)


def groups_of(d, o, groups):
    return {((r + d * o) // GROUP) % groups for r in range(GROUP)}


def far_first(steps):
    return sorted(list(steps) + [(0, 0)], key=lambda n: (-n[1], -n[0]))


def make_order(steps, zs):
    arrival = {n: FIRST + NEXT * i for i, n in enumerate(far_first(steps))}
    kids = {}
    for (d, o), s in steps.items():
        kids.setdefault((d, o - s) if o - s else (0, 0), []).append((d, o))
    ready = {}
    left = {n: len(kids.get(n, [])) for n in steps}
    at = {n: arrival[n] for n in steps}
    events = [(at[n], n, 0) for n in steps if not left[n]]
    free = {1: 0.0, -1: 0.0}
    while events:
        events.sort()
        t, n, hop = events.pop(0)
        step = steps[n]
        if hop == 0:
            ready[n] = t + (SLACK if n in kids else 0.0)
        if hop < abs(step):
            link = n[0] if step > 0 else -n[0]
            begin = max(t, free[link])
            free[link] = begin + WIRE
            last = hop + 1 == abs(step)
            events.append((begin + HOP + (WIRE + STOP if last else 0.0), n, hop + 1))
            continue
        up = (n[0], n[1] - step)
        if up[1]:
            left[up] -= 1
            at[up] = max(at[up], t)
            if not left[up]:
                events.append((at[up], up, 0))
    return sorted(steps, key=lambda n: (ready[n], -n[1], -n[0])), kids


def kernel(
    nw,
    zs,
    counts_h,
    frag_ref,
    params_h,
    first_h,
    second_h,
    glob_h,
    mom_h,
    feats_h,
    cot_h,
    result,
    counts,
    feats,
    cot,
    params,
    first,
    second,
    glob,
    mom,
    term,
    crecv,
    chip,
    xrecv,
    own,
    zsend,
    zrecv,
    drift,
    wall,
    spread,
    load_sem,
    csend_sem,
    crecv_sem,
    xsend_sem,
    xrecv_sem,
    zsend_sem,
    zrecv_sem,
    wsend_sem,
    wrecv_sem,
    far_sem,
):
    w = lax.axis_index("worker")
    k = lax.axis_index("fsdp")
    xh = k // (2 * zs)
    z = (k // 2) % zs
    c = k % 2
    rows = params.shape[0]
    tokens = feats.shape[0]
    groups = zs // GROUP

    steps = make_tree(zs)
    order, kids = make_order(steps, zs)
    slot = {}
    leaves, trunk = {}, {}
    for up, kin in kids.items():
        leaves[up] = [n for n in kin if n not in kids]
        trunk[up] = [n for n in kin if n in kids]
        for node in leaves[up] + trunk[up]:
            slot[node] = len(slot)
    channel = {up: i for i, up in enumerate(kids)}
    for kin in trunk.values():
        for node in kin:
            channel[node, 0], channel[node, 1] = len(channel), len(channel) + 1
    def at(x, zz, core):
        return (w, x * (2 * zs) + zz * 2 + core)

    core_mate = at(xh, z, 1 - c)
    x_mate = at(1 - xh, z, c)

    def z_mate(hop):
        return at(xh, (z + hop + zs) % zs, c)

    y, xl, ny = w // 2, w % 2, nw // 2
    side_mate = (2 * y + 1 - xl, k)
    up_mate, down_mate = (2 * ((y + 1) % ny) + xl, k), (2 * ((y + ny - 1) % ny) + xl, k)
    partners = [core_mate, x_mate] + [z_mate(h) for h in (1, -1, NEAR, -NEAR)]
    if nw > 1:
        partners.append(side_mate)
    if ny > 1:
        partners += [up_mate, down_mate]
    barrier = pltpu.get_barrier_semaphore()
    for mate in partners:
        pl.semaphore_signal(barrier, inc=1, device_id=mate, device_id_type=MESH)

    loads = []
    for i, (src, dst) in enumerate(
        (
            (cot_h, cot),
            (feats_h, feats),
            (counts_h, counts),
            (params_h, params),
            (glob_h, glob),
            (first_h, first),
            (second_h, second),
            (mom_h, mom),
        )
    ):
        copy = pltpu.make_async_copy(src, dst, load_sem.at[min(i, 3)])
        copy.start()
        loads.append(copy)

    loads[2].wait()
    live = counts[w]
    live_f = live.astype(F32)
    loads[0].wait()
    position = k * tokens + lax.broadcasted_iota(jnp.int32, cot.shape, 0)
    masked = jnp.where(position < live, cot[...], jnp.zeros_like(cot[...]))
    loads[1].wait()

    def group_z(i):
        return ((z // GROUP + turn(i, groups)) % groups) * GROUP

    def remote(src, dst, send, recv, mate):
        return pltpu.make_async_remote_copy(
            src_ref=src, dst_ref=dst, send_sem=send, recv_sem=recv, device_id=mate, device_id_type=MESH
        )

    core_done, reduced = set(), set()

    def multiply(i):
        base = group_z(i)
        for x in range(2):
            for pair in range(GROUP // 2):
                col = pl.multiple_of((x * zs + base + 2 * pair) * (2 * rows), 4 * rows)
                block = lax.dot_general(
                    feats[:, pl.ds(col, 4 * rows)],
                    masked,
                    (((0,), (0,)), ((), ())),
                    preferred_element_type=F32,
                )
                for dz in range(2):
                    for core in range(2):
                        lo = (2 * dz + core) * rows
                        term[core, x, base + 2 * pair + dz] = block[lo : lo + rows]

    def send_core(i):
        zr = pl.ds(group_z(i), GROUP)
        copy = remote(term.at[1 - c, :, zr], crecv.at[:, zr], csend_sem, crecv_sem.at[part_of(CORE_PARTS, i)], core_mate)
        copy.start()

    far = far_first(steps)

    def z_of(node):
        return (z + node[0] * node[1] + zs) % zs

    def reduce_pair(i):
        part = part_of(CORE_PARTS, i)
        if part not in core_done:
            core_done.add(part)
            wait_core(part)
        zr = pl.ds(group_z(i), GROUP)
        chip[:, zr] = term[c, :, zr] + crecv[:, zr]

    def send_x(i):
        where = groups_of(*far[i], groups)
        for j in range(groups):
            if turn(j, groups) in where and j not in reduced:
                reduced.add(j)
                reduce_pair(j)
        zz = z_of(far[i])
        remote(chip.at[1 - xh, zz], xrecv.at[zz], xsend_sem, xrecv_sem.at[part_of(X_PARTS, i)], x_mate).start()

    def wait_core(part):
        n = GROUP * (CORE_PARTS[part + 1] - CORE_PARTS[part])
        zr = pl.ds(0, n)
        remote(term.at[1 - c, :, zr], crecv.at[:, zr], csend_sem, crecv_sem.at[part], core_mate).wait_recv()

    def wait_x(part):
        zr = pl.ds(0, X_PARTS[part + 1] - X_PARTS[part])
        remote(chip.at[1 - xh, zr], xrecv.at[zr], xsend_sem, xrecv_sem.at[part], x_mate).wait_recv()

    for i in range(groups):
        multiply(i)

    pltpu.make_async_copy(result, result, load_sem.at[3]).wait()
    frag = frag_ref[0]
    old = params[pl.ds(0, rows // FRAGS, stride=FRAGS), :]
    for f in range(1, FRAGS):
        old = jnp.where(frag == f, params[pl.ds(f, rows // FRAGS, stride=FRAGS), :], old)
    mine = live_f * (glob[...] - old)
    drift[...] = mine
    wall[w] = mine

    pl.semaphore_wait(barrier, len(partners))
    for i in range(groups):
        send_core(i)
    for h in (NEAR, -NEAR):
        pl.semaphore_signal(far_sem, inc=1, device_id=z_mate(h), device_id_type=MESH)
    if nw > 1:
        remote(drift, wall.at[w], wsend_sem.at[0], wrecv_sem.at[0], side_mate).start()
    for i in range(zs):
        send_x(i)

    def block(i):
        return wall.at[pl.ds(2 * ((y + i + ny) % ny), 2)]

    def worker_pairs():
        if nw > 1:
            remote(drift, drift, wsend_sem.at[0], wrecv_sem.at[0], side_mate).wait_recv()
        if ny > 1:
            remote(block(0), block(0), wsend_sem.at[1], wrecv_sem.at[1], up_mate).start()
            remote(block(0), block(0), wsend_sem.at[2], wrecv_sem.at[2], down_mate).start()

    def worker_relay():
        if ny > 1:
            remote(block(-1), block(-1), wsend_sem.at[0], wrecv_sem.at[1], up_mate).wait_recv()
            remote(block(-1), block(-1), wsend_sem.at[3], wrecv_sem.at[3], up_mate).start()

    def outer():
        if ny > 1:
            remote(block(1), block(1), wsend_sem.at[0], wrecv_sem.at[2], down_mate).wait_recv()
            remote(block(2), block(2), wsend_sem.at[0], wrecv_sem.at[3], up_mate).wait_recv()
        total = wall[0]
        token_total = counts[0]
        for i in range(1, nw):
            total = total + wall[i]
            token_total = token_total + counts[i]
        pseudo = total / token_total.astype(F32)
        momentum = NESTEROV * mom[...] + pseudo
        fresh = glob[...] - OUTER_RATE * (pseudo + NESTEROV * momentum)
        result[pl.ds(3 * rows + fresh.shape[0], fresh.shape[0]), :] = momentum
        result[pl.ds(3 * rows, fresh.shape[0]), :] = fresh
        for f in range(FRAGS):
            spread[pl.ds(f, rows // FRAGS, stride=FRAGS), :] = fresh

    done = set()

    def need(node):
        part = part_of(X_PARTS, far.index(node))
        if part not in done:
            done.add(part)
            wait_x(part)
            for other in far[X_PARTS[part] : X_PARTS[part + 1]]:
                zz = z_of(other)
                own[zz] = chip[xh, zz] + xrecv[zz]

    def gather(node, zz):
        kin = leaves[node]
        zr = pl.ds(slot[kin[0]], len(kin))
        remote(zrecv.at[zr], zrecv.at[zr], zsend_sem, zrecv_sem.at[channel[node]], x_mate).wait_recv()
        total = own[zz]
        for kid in kin:
            total = total + zrecv[slot[kid]]
        for half in range(2):
            hr = pl.ds(half * (rows // 2), rows // 2)
            part = total[half * (rows // 2) : (half + 1) * (rows // 2)]
            for kid in trunk[node]:
                piece = zrecv.at[slot[kid], hr]
                remote(piece, piece, zsend_sem, zrecv_sem.at[channel[kid, half]], x_mate).wait_recv()
                part = part + zrecv[slot[kid], hr]
            yield hr, half, part

    worker_pairs()
    pl.semaphore_wait(far_sem, 2)
    for count, node in enumerate(order):
        d, o = node
        need(node)
        zz = z_of(node)
        i = slot[node]
        up = (d, o - steps[node]) if o - steps[node] else (0, 0)
        mate = z_mate(d * steps[node])
        if node in kids:
            for hr, half, part in gather(node, zz):
                zsend[i, hr] = part
                sem = zrecv_sem.at[channel[node, half]]
                remote(zsend.at[i, hr], zrecv.at[i, hr], zsend_sem, sem, mate).start()
        else:
            remote(own.at[zz], zrecv.at[i], zsend_sem, zrecv_sem.at[channel[up]], mate).start()
        if count == 4:
            worker_relay()

    need((0, 0))
    outer()
    gradient = jnp.concatenate([part for _, _, part in gather((0, 0), z)]) / live_f
    first_new = BETA_ONE * first[...] + (1.0 - BETA_ONE) * gradient
    second_new = BETA_TWO * second[...] + (1.0 - BETA_TWO) * gradient * gradient
    update = first_new / CORRECT_ONE / (jnp.sqrt(second_new / CORRECT_TWO) + ADAM_EPS)
    before = params[...]
    inner = before - LEARN_RATE * (update + DECAY_RATE * before)
    chosen = lax.broadcasted_iota(jnp.int32, inner.shape, 0) % FRAGS == frag
    result[pl.ds(0, rows), :] = jnp.where(chosen, MIXING * spread[...] + (1.0 - MIXING) * inner, inner)
    result[pl.ds(rows, rows), :] = first_new
    result[pl.ds(2 * rows, rows), :] = second_new

    remote(crecv, crecv, csend_sem, crecv_sem.at[0], core_mate).wait_send()
    remote(xrecv, xrecv, xsend_sem, xrecv_sem.at[0], x_mate).wait_send()
    remote(zrecv, zrecv, zsend_sem, zrecv_sem.at[0], x_mate).wait_send()
    if nw > 1:
        remote(drift, drift, wsend_sem.at[0], wrecv_sem.at[0], side_mate).wait_send()
    for i in range(1, 4 if ny > 1 else 0):
        remote(block(0), block(0), wsend_sem.at[i], wrecv_sem.at[i], up_mate).wait_send()


def hand_out(packed, *refs):
    outs, sems = refs[:-1], refs[-1]
    copies, lo = [], 0
    for i, out in enumerate(outs):
        n = out.shape[0]
        copy = pltpu.make_async_copy(packed.at[pl.ds(lo, n)], out, sems.at[i])
        copy.start()
        copies.append(copy)
        lo += n
    for copy in copies:
        copy.wait()


def solution(mesh):
    nw = mesh.shape["worker"]
    zs = mesh.shape["fsdp"] // 4

    def step(params, first, second, glob, mom, features, cotangent, counts, frag):
        rows, width = params.shape[1:]
        frows = glob.shape[0]
        tokens, depth = features.shape[1:]
        vm = pltpu.VMEM
        dma = pltpu.SemaphoreType.DMA
        messages = zs - 1
        stops = 3 * len(make_order(make_tree(zs), zs)[1])
        groups = zs // GROUP
        tile = (rows, width)
        in_hbm = functools.partial(pltpu.with_memory_space_constraint, memory_space=pltpu.HBM)
        big = jax.ShapeDtypeStruct(tile, F32)
        small = jax.ShapeDtypeStruct((frows, width), F32)
        hbm = pl.BlockSpec(memory_space=pl.ANY)
        packed = pl.pallas_call(
            functools.partial(kernel, nw, zs),
            out_shape=jax.ShapeDtypeStruct((3 * rows + 2 * frows, width), F32),
            in_specs=[hbm, pl.BlockSpec(memory_space=pltpu.SMEM)] + [hbm] * 7,
            out_specs=pl.BlockSpec(memory_space=vm),
            scratch_shapes=[
                pltpu.SMEM((nw,), jnp.int32),
                vm((tokens, depth), jnp.bfloat16),
                vm((tokens, width), jnp.bfloat16),
                vm(tile, F32),
                vm(tile, F32),
                vm(tile, F32),
                vm((frows, width), F32),
                vm((frows, width), F32),
                vm((2, 2, zs) + tile, F32),
                vm((2, zs) + tile, F32),
                vm((2, zs) + tile, F32),
                vm((zs,) + tile, F32),
                vm((zs,) + tile, F32),
                vm((messages,) + tile, F32),
                vm((messages,) + tile, F32),
                vm((frows, width), F32),
                vm((nw, frows, width), F32),
                vm(tile, F32),
                dma((4,)),
                dma(()),
                dma((len(CORE_PARTS) - 1,)),
                dma(()),
                dma((len(X_PARTS) - 1,)),
                dma(()),
                dma((stops,)),
                dma((4,)),
                dma((4,)),
                pltpu.SemaphoreType.REGULAR,
            ],
            compiler_params=pltpu.CompilerParams(collective_id=0, has_side_effects=True, vmem_limit_bytes=VMEM_LIMIT),
            name="diloco_step",
        )(in_hbm(counts), frag, *map(in_hbm, (params[0], first[0], second[0], glob, mom, features[0], cotangent[0])))
        out = pl.pallas_call(
            hand_out,
            out_shape=(big, big, big, small, small),
            in_specs=[hbm],
            out_specs=[hbm] * 5,
            scratch_shapes=[dma((5,))],
            compiler_params=pltpu.CompilerParams(vmem_limit_bytes=1024 * 1024),
            name="hand_out",
        )(packed)
        return (out[0][None], out[1][None], out[2][None], out[3], out[4])

    held = P("worker", "fsdp", None)
    shared = P("fsdp", None)
    return jax.shard_map(
        step,
        mesh=mesh,
        in_specs=(held, held, held, shared, shared, held, held, P(), P()),
        out_specs=(held, held, held, shared, shared),
        check_vma=False,
    )
```

```python
import functools

import jax
import jax.numpy as jnp
from jax import lax
from jax.experimental import pallas as pl
from jax.experimental.pallas import tpu as pltpu
from jax.sharding import PartitionSpec as P

MESH = pl.DeviceIdType.MESH
F32 = jnp.float32

FRAGS = 4
BETA_ONE = 0.9
BETA_TWO = 0.95
CORRECT_ONE = 0.6513216
CORRECT_TWO = 0.401263
ADAM_EPS = 1e-08
LEARN_RATE = 0.02
DECAY_RATE = 0.1
NESTEROV = 0.9
OUTER_RATE = 0.7
MIXING = 0.5

VMEM_LIMIT = 16 * 1024 * 1024
GROUP = 2
CORE_PARTS = (0, 1, 2, 4, 8, 16)
X_PARTS = tuple(range(9)) + (10, 12, 14, 16, 18, 20, 24, 28, 32)
STOPS = {1: (12, 8, 4), -1: (12, 8, 4)}
NEAR = 2

HOP, WIRE, STOP, FIRST, NEXT, SLACK = 0.78, 0.35, 0.88, 5.0, 0.36, -0.7


def make_tree(zs):
    steps = {}
    for d, length in ((1, zs // 2), (-1, zs - zs // 2 - 1)):
        stops = [0] + [s for s in STOPS[d] if s <= length]
        for o in range(1, length + 1):
            if o in stops:
                steps[d, o] = o - max(s for s in stops if s < o)
            else:
                steps[d, o] = o - min(stops, key=lambda s: (abs(s - o), s))
    return steps


def turn(i, groups):
    return (groups // 2 + ((i + 1) // 2) * (1 if i % 2 else -1)) % groups


def part_of(bounds, i):
    return max(p for p, first in enumerate(bounds) if first <= i)


def groups_of(d, o, groups):
    return {((r + d * o) // GROUP) % groups for r in range(GROUP)}


def far_first(steps):
    return sorted(list(steps) + [(0, 0)], key=lambda n: (-n[1], -n[0]))


def make_order(steps, zs):
    arrival = {n: FIRST + NEXT * i for i, n in enumerate(far_first(steps))}
    kids = {}
    for (d, o), s in steps.items():
        kids.setdefault((d, o - s) if o - s else (0, 0), []).append((d, o))
    ready = {}
    left = {n: len(kids.get(n, [])) for n in steps}
    at = {n: arrival[n] for n in steps}
    events = [(at[n], n, 0) for n in steps if not left[n]]
    free = {1: 0.0, -1: 0.0}
    while events:
        events.sort()
        t, n, hop = events.pop(0)
        step = steps[n]
        if hop == 0:
            ready[n] = t + (SLACK if n in kids else 0.0)
        if hop < abs(step):
            link = n[0] if step > 0 else -n[0]
            begin = max(t, free[link])
            free[link] = begin + WIRE
            last = hop + 1 == abs(step)
            events.append((begin + HOP + (WIRE + STOP if last else 0.0), n, hop + 1))
            continue
        up = (n[0], n[1] - step)
        if up[1]:
            left[up] -= 1
            at[up] = max(at[up], t)
            if not left[up]:
                events.append((at[up], up, 0))
    return sorted(steps, key=lambda n: (ready[n], -n[1], -n[0])), kids


def kernel(
    nw,
    zs,
    counts_h,
    frag_ref,
    params_h,
    first_h,
    second_h,
    glob_h,
    mom_h,
    feats_h,
    cot_h,
    result,
    counts,
    feats,
    cot,
    params,
    first,
    second,
    glob,
    mom,
    term,
    crecv,
    chip,
    xrecv,
    own,
    zsend,
    zrecv,
    drift,
    wall,
    spread,
    load_sem,
    csend_sem,
    crecv_sem,
    xsend_sem,
    xrecv_sem,
    zsend_sem,
    zrecv_sem,
    wsend_sem,
    wrecv_sem,
    far_sem,
):
    w = lax.axis_index("worker")
    k = lax.axis_index("fsdp")
    xh = k // (2 * zs)
    z = (k // 2) % zs
    c = k % 2
    rows = params.shape[0]
    tokens = feats.shape[0]
    groups = zs // GROUP

    steps = make_tree(zs)
    order, kids = make_order(steps, zs)
    slot = {}
    leaves, trunk = {}, {}
    for up, kin in kids.items():
        leaves[up] = [n for n in kin if n not in kids]
        trunk[up] = [n for n in kin if n in kids]
        for node in leaves[up] + trunk[up]:
            slot[node] = len(slot)
    channel = {up: i for i, up in enumerate(kids)}
    for kin in trunk.values():
        for node in kin:
            channel[node, 0], channel[node, 1] = len(channel), len(channel) + 1
    def at(x, zz, core):
        return (w, x * (2 * zs) + zz * 2 + core)

    core_mate = at(xh, z, 1 - c)
    x_mate = at(1 - xh, z, c)

    def z_mate(hop):
        return at(xh, (z + hop + zs) % zs, c)

    y, xl, ny = w // 2, w % 2, nw // 2
    side_mate = (2 * y + 1 - xl, k)
    up_mate, down_mate = (2 * ((y + 1) % ny) + xl, k), (2 * ((y + ny - 1) % ny) + xl, k)
    partners = [core_mate, x_mate] + [z_mate(h) for h in (1, -1, NEAR, -NEAR)]
    if nw > 1:
        partners.append(side_mate)
    if ny > 1:
        partners += [up_mate, down_mate]
    barrier = pltpu.get_barrier_semaphore()
    for mate in partners:
        pl.semaphore_signal(barrier, inc=1, device_id=mate, device_id_type=MESH)

    loads = []
    for i, (src, dst) in enumerate(
        (
            (cot_h, cot),
            (feats_h, feats),
            (counts_h, counts),
            (params_h, params),
            (glob_h, glob),
            (first_h, first),
            (second_h, second),
            (mom_h, mom),
        )
    ):
        copy = pltpu.make_async_copy(src, dst, load_sem.at[min(i, 3)])
        copy.start()
        loads.append(copy)

    loads[2].wait()
    live = counts[w]
    live_f = live.astype(F32)
    loads[0].wait()
    position = k * tokens + lax.broadcasted_iota(jnp.int32, cot.shape, 0)
    masked = jnp.where(position < live, cot[...], jnp.zeros_like(cot[...]))
    loads[1].wait()

    def group_z(i):
        return ((z // GROUP + turn(i, groups)) % groups) * GROUP

    def remote(src, dst, send, recv, mate):
        return pltpu.make_async_remote_copy(
            src_ref=src, dst_ref=dst, send_sem=send, recv_sem=recv, device_id=mate, device_id_type=MESH
        )

    core_done, reduced = set(), set()

    def multiply(i):
        base = group_z(i)
        for x in range(2):
            for pair in range(GROUP // 2):
                col = pl.multiple_of((x * zs + base + 2 * pair) * (2 * rows), 4 * rows)
                block = lax.dot_general(
                    feats[:, pl.ds(col, 4 * rows)],
                    masked,
                    (((0,), (0,)), ((), ())),
                    preferred_element_type=F32,
                )
                for dz in range(2):
                    for core in range(2):
                        lo = (2 * dz + core) * rows
                        term[core, x, base + 2 * pair + dz] = block[lo : lo + rows]

    def send_core(i):
        zr = pl.ds(group_z(i), GROUP)
        copy = remote(term.at[1 - c, :, zr], crecv.at[:, zr], csend_sem, crecv_sem.at[part_of(CORE_PARTS, i)], core_mate)
        copy.start()

    far = far_first(steps)

    def z_of(node):
        return (z + node[0] * node[1] + zs) % zs

    def reduce_pair(i):
        part = part_of(CORE_PARTS, i)
        if part not in core_done:
            core_done.add(part)
            wait_core(part)
        zr = pl.ds(group_z(i), GROUP)
        chip[:, zr] = term[c, :, zr] + crecv[:, zr]

    def send_x(i):
        where = groups_of(*far[i], groups)
        for j in range(groups):
            if turn(j, groups) in where and j not in reduced:
                reduced.add(j)
                reduce_pair(j)
        zz = z_of(far[i])
        remote(chip.at[1 - xh, zz], xrecv.at[zz], xsend_sem, xrecv_sem.at[part_of(X_PARTS, i)], x_mate).start()

    def wait_core(part):
        n = GROUP * (CORE_PARTS[part + 1] - CORE_PARTS[part])
        zr = pl.ds(0, n)
        remote(term.at[1 - c, :, zr], crecv.at[:, zr], csend_sem, crecv_sem.at[part], core_mate).wait_recv()

    def wait_x(part):
        zr = pl.ds(0, X_PARTS[part + 1] - X_PARTS[part])
        remote(chip.at[1 - xh, zr], xrecv.at[zr], xsend_sem, xrecv_sem.at[part], x_mate).wait_recv()

    for i in range(groups):
        multiply(i)

    pltpu.make_async_copy(result, result, load_sem.at[3]).wait()
    frag = frag_ref[0]
    old = params[pl.ds(0, rows // FRAGS, stride=FRAGS), :]
    for f in range(1, FRAGS):
        old = jnp.where(frag == f, params[pl.ds(f, rows // FRAGS, stride=FRAGS), :], old)
    mine = live_f * (glob[...] - old)
    drift[...] = mine
    wall[w] = mine

    pl.semaphore_wait(barrier, len(partners))
    for i in range(groups):
        send_core(i)
    for h in (NEAR, -NEAR):
        pl.semaphore_signal(far_sem, inc=1, device_id=z_mate(h), device_id_type=MESH)
    if nw > 1:
        remote(drift, wall.at[w], wsend_sem.at[0], wrecv_sem.at[0], side_mate).start()
    for i in range(zs):
        send_x(i)

    def block(i):
        return wall.at[pl.ds(2 * ((y + i + ny) % ny), 2)]

    def worker_pairs():
        if nw > 1:
            remote(drift, drift, wsend_sem.at[0], wrecv_sem.at[0], side_mate).wait_recv()
        if ny > 1:
            remote(block(0), block(0), wsend_sem.at[1], wrecv_sem.at[1], up_mate).start()
            remote(block(0), block(0), wsend_sem.at[2], wrecv_sem.at[2], down_mate).start()

    def worker_relay():
        if ny > 1:
            remote(block(-1), block(-1), wsend_sem.at[0], wrecv_sem.at[1], up_mate).wait_recv()
            remote(block(-1), block(-1), wsend_sem.at[3], wrecv_sem.at[3], up_mate).start()

    def outer():
        if ny > 1:
            remote(block(1), block(1), wsend_sem.at[0], wrecv_sem.at[2], down_mate).wait_recv()
            remote(block(2), block(2), wsend_sem.at[0], wrecv_sem.at[3], up_mate).wait_recv()
        total = wall[0]
        token_total = counts[0]
        for i in range(1, nw):
            total = total + wall[i]
            token_total = token_total + counts[i]
        pseudo = total / token_total.astype(F32)
        momentum = NESTEROV * mom[...] + pseudo
        fresh = glob[...] - OUTER_RATE * (pseudo + NESTEROV * momentum)
        result[pl.ds(3 * rows + fresh.shape[0], fresh.shape[0]), :] = momentum
        result[pl.ds(3 * rows, fresh.shape[0]), :] = fresh
        for f in range(FRAGS):
            spread[pl.ds(f, rows // FRAGS, stride=FRAGS), :] = fresh

    done = set()

    def need(node):
        part = part_of(X_PARTS, far.index(node))
        if part not in done:
            done.add(part)
            wait_x(part)
            for other in far[X_PARTS[part] : X_PARTS[part + 1]]:
                zz = z_of(other)
                own[zz] = chip[xh, zz] + xrecv[zz]

    def gather(node, zz):
        kin = leaves[node]
        zr = pl.ds(slot[kin[0]], len(kin))
        remote(zrecv.at[zr], zrecv.at[zr], zsend_sem, zrecv_sem.at[channel[node]], x_mate).wait_recv()
        total = own[zz]
        for kid in kin:
            total = total + zrecv[slot[kid]]
        for half in range(2):
            hr = pl.ds(half * (rows // 2), rows // 2)
            part = total[half * (rows // 2) : (half + 1) * (rows // 2)]
            for kid in trunk[node]:
                piece = zrecv.at[slot[kid], hr]
                remote(piece, piece, zsend_sem, zrecv_sem.at[channel[kid, half]], x_mate).wait_recv()
                part = part + zrecv[slot[kid], hr]
            yield hr, half, part

    worker_pairs()
    pl.semaphore_wait(far_sem, 2)
    for count, node in enumerate(order):
        d, o = node
        need(node)
        zz = z_of(node)
        i = slot[node]
        up = (d, o - steps[node]) if o - steps[node] else (0, 0)
        mate = z_mate(d * steps[node])
        if node in kids:
            for hr, half, part in gather(node, zz):
                zsend[i, hr] = part
                sem = zrecv_sem.at[channel[node, half]]
                remote(zsend.at[i, hr], zrecv.at[i, hr], zsend_sem, sem, mate).start()
        else:
            remote(own.at[zz], zrecv.at[i], zsend_sem, zrecv_sem.at[channel[up]], mate).start()
        if count == 4:
            worker_relay()

    need((0, 0))
    outer()
    gradient = jnp.concatenate([part for _, _, part in gather((0, 0), z)]) / live_f
    first_new = BETA_ONE * first[...] + (1.0 - BETA_ONE) * gradient
    second_new = BETA_TWO * second[...] + (1.0 - BETA_TWO) * gradient * gradient
    update = first_new / CORRECT_ONE / (jnp.sqrt(second_new / CORRECT_TWO) + ADAM_EPS)
    before = params[...]
    inner = before - LEARN_RATE * (update + DECAY_RATE * before)
    chosen = lax.broadcasted_iota(jnp.int32, inner.shape, 0) % FRAGS == frag
    result[pl.ds(0, rows), :] = jnp.where(chosen, MIXING * spread[...] + (1.0 - MIXING) * inner, inner)
    result[pl.ds(rows, rows), :] = first_new
    result[pl.ds(2 * rows, rows), :] = second_new

    remote(crecv, crecv, csend_sem, crecv_sem.at[0], core_mate).wait_send()
    remote(xrecv, xrecv, xsend_sem, xrecv_sem.at[0], x_mate).wait_send()
    remote(zrecv, zrecv, zsend_sem, zrecv_sem.at[0], x_mate).wait_send()
    if nw > 1:
        remote(drift, drift, wsend_sem.at[0], wrecv_sem.at[0], side_mate).wait_send()
    for i in range(1, 4 if ny > 1 else 0):
        remote(block(0), block(0), wsend_sem.at[i], wrecv_sem.at[i], up_mate).wait_send()


def hand_out(packed, *refs):
    outs, sems = refs[:-1], refs[-1]
    copies, lo = [], 0
    for i, out in enumerate(outs):
        n = out.shape[0]
        copy = pltpu.make_async_copy(packed.at[pl.ds(lo, n)], out, sems.at[i])
        copy.start()
        copies.append(copy)
        lo += n
    for copy in copies:
        copy.wait()


def solution(mesh):
    nw = mesh.shape["worker"]
    zs = mesh.shape["fsdp"] // 4

    def step(params, first, second, glob, mom, features, cotangent, counts, frag):
        rows, width = params.shape[1:]
        frows = glob.shape[0]
        tokens, depth = features.shape[1:]
        vm = pltpu.VMEM
        dma = pltpu.SemaphoreType.DMA
        messages = zs - 1
        stops = 3 * len(make_order(make_tree(zs), zs)[1])
        groups = zs // GROUP
        tile = (rows, width)
        in_hbm = functools.partial(pltpu.with_memory_space_constraint, memory_space=pltpu.HBM)
        big = jax.ShapeDtypeStruct(tile, F32)
        small = jax.ShapeDtypeStruct((frows, width), F32)
        hbm = pl.BlockSpec(memory_space=pl.ANY)
        packed = pl.pallas_call(
            functools.partial(kernel, nw, zs),
            out_shape=jax.ShapeDtypeStruct((3 * rows + 2 * frows, width), F32),
            in_specs=[hbm, pl.BlockSpec(memory_space=pltpu.SMEM)] + [hbm] * 7,
            out_specs=pl.BlockSpec(memory_space=vm),
            scratch_shapes=[
                pltpu.SMEM((nw,), jnp.int32),
                vm((tokens, depth), jnp.bfloat16),
                vm((tokens, width), jnp.bfloat16),
                vm(tile, F32),
                vm(tile, F32),
                vm(tile, F32),
                vm((frows, width), F32),
                vm((frows, width), F32),
                vm((2, 2, zs) + tile, F32),
                vm((2, zs) + tile, F32),
                vm((2, zs) + tile, F32),
                vm((zs,) + tile, F32),
                vm((zs,) + tile, F32),
                vm((messages,) + tile, F32),
                vm((messages,) + tile, F32),
                vm((frows, width), F32),
                vm((nw, frows, width), F32),
                vm(tile, F32),
                dma((4,)),
                dma(()),
                dma((len(CORE_PARTS) - 1,)),
                dma(()),
                dma((len(X_PARTS) - 1,)),
                dma(()),
                dma((stops,)),
                dma((4,)),
                dma((4,)),
                pltpu.SemaphoreType.REGULAR,
            ],
            compiler_params=pltpu.CompilerParams(collective_id=0, has_side_effects=True, vmem_limit_bytes=VMEM_LIMIT),
            name="diloco_step",
        )(in_hbm(counts), frag, *map(in_hbm, (params[0], first[0], second[0], glob, mom, features[0], cotangent[0])))
        out = pl.pallas_call(
            hand_out,
            out_shape=(big, big, big, small, small),
            in_specs=[hbm],
            out_specs=[hbm] * 5,
            scratch_shapes=[dma((5,))],
            compiler_params=pltpu.CompilerParams(vmem_limit_bytes=1024 * 1024),
            name="hand_out",
        )(packed)
        return (out[0][None], out[1][None], out[2][None], out[3], out[4])

    held = P("worker", "fsdp", None)
    shared = P("fsdp", None)
    return jax.shard_map(
        step,
        mesh=mesh,
        in_specs=(held, held, held, shared, shared, held, held, P(), P()),
        out_specs=(held, held, held, shared, shared),
        check_vma=False,
    )
```

```python
import functools

import jax
import jax.numpy as jnp
from jax import lax
from jax.experimental import pallas as pl
from jax.experimental.pallas import tpu as pltpu
from jax.sharding import PartitionSpec as P

MESH = pl.DeviceIdType.MESH
F32 = jnp.float32

FRAGS = 4
BETA_ONE = 0.9
BETA_TWO = 0.95
CORRECT_ONE = 0.6513216
CORRECT_TWO = 0.401263
ADAM_EPS = 1e-08
LEARN_RATE = 0.02
DECAY_RATE = 0.1
NESTEROV = 0.9
OUTER_RATE = 0.7
MIXING = 0.5

VMEM_LIMIT = 16 * 1024 * 1024
GROUP = 2
CORE_PARTS = (0, 1, 2, 4, 8, 16)
X_PARTS = tuple(range(9)) + (10, 12, 14, 16, 18, 20, 24, 28, 32)
STOPS = {1: (12, 8, 4), -1: (11, 7, 4)}
NEAR = 2

HOP, WIRE, STOP, FIRST, NEXT, SLACK = 0.78, 0.35, 0.88, 5.0, 0.36, -0.7


def make_tree(zs):
    steps = {}
    for d, length in ((1, zs // 2), (-1, zs - zs // 2 - 1)):
        stops = [0] + [s for s in STOPS[d] if s <= length]
        for o in range(1, length + 1):
            if o in stops:
                steps[d, o] = o - max(s for s in stops if s < o)
            else:
                steps[d, o] = o - min(stops, key=lambda s: (abs(s - o), s))
    return steps


def turn(i, groups):
    return (groups // 2 + ((i + 1) // 2) * (1 if i % 2 else -1)) % groups


def part_of(bounds, i):
    return max(p for p, first in enumerate(bounds) if first <= i)


def groups_of(d, o, groups):
    return {((r + d * o) // GROUP) % groups for r in range(GROUP)}


def far_first(steps):
    return sorted(list(steps) + [(0, 0)], key=lambda n: (-n[1], -n[0]))


def make_order(steps, zs):
    arrival = {n: FIRST + NEXT * i for i, n in enumerate(far_first(steps))}
    kids = {}
    for (d, o), s in steps.items():
        kids.setdefault((d, o - s) if o - s else (0, 0), []).append((d, o))
    ready = {}
    left = {n: len(kids.get(n, [])) for n in steps}
    at = {n: arrival[n] for n in steps}
    events = [(at[n], n, 0) for n in steps if not left[n]]
    free = {1: 0.0, -1: 0.0}
    while events:
        events.sort()
        t, n, hop = events.pop(0)
        step = steps[n]
        if hop == 0:
            ready[n] = t + (SLACK if n in kids else 0.0)
        if hop < abs(step):
            link = n[0] if step > 0 else -n[0]
            begin = max(t, free[link])
            free[link] = begin + WIRE
            last = hop + 1 == abs(step)
            events.append((begin + HOP + (WIRE + STOP if last else 0.0), n, hop + 1))
            continue
        up = (n[0], n[1] - step)
        if up[1]:
            left[up] -= 1
            at[up] = max(at[up], t)
            if not left[up]:
                events.append((at[up], up, 0))
    return sorted(steps, key=lambda n: (ready[n], -n[1], -n[0])), kids


def kernel(
    nw,
    zs,
    counts_h,
    frag_ref,
    params_h,
    first_h,
    second_h,
    glob_h,
    mom_h,
    feats_h,
    cot_h,
    result,
    counts,
    feats,
    cot,
    params,
    first,
    second,
    glob,
    mom,
    term,
    crecv,
    chip,
    xrecv,
    own,
    zsend,
    zrecv,
    drift,
    wall,
    spread,
    load_sem,
    csend_sem,
    crecv_sem,
    xsend_sem,
    xrecv_sem,
    zsend_sem,
    zrecv_sem,
    wsend_sem,
    wrecv_sem,
    far_sem,
):
    w = lax.axis_index("worker")
    k = lax.axis_index("fsdp")
    xh = k // (2 * zs)
    z = (k // 2) % zs
    c = k % 2
    rows = params.shape[0]
    tokens = feats.shape[0]
    groups = zs // GROUP

    steps = make_tree(zs)
    order, kids = make_order(steps, zs)
    slot = {}
    leaves, trunk = {}, {}
    for up, kin in kids.items():
        leaves[up] = [n for n in kin if n not in kids]
        trunk[up] = [n for n in kin if n in kids]
        for node in leaves[up] + trunk[up]:
            slot[node] = len(slot)
    channel = {up: i for i, up in enumerate(kids)}
    for kin in trunk.values():
        for node in kin:
            channel[node, 0], channel[node, 1] = len(channel), len(channel) + 1
    def at(x, zz, core):
        return (w, x * (2 * zs) + zz * 2 + core)

    core_mate = at(xh, z, 1 - c)
    x_mate = at(1 - xh, z, c)

    def z_mate(hop):
        return at(xh, (z + hop + zs) % zs, c)

    y, xl, ny = w // 2, w % 2, nw // 2
    side_mate = (2 * y + 1 - xl, k)
    up_mate, down_mate = (2 * ((y + 1) % ny) + xl, k), (2 * ((y + ny - 1) % ny) + xl, k)
    partners = [core_mate, x_mate] + [z_mate(h) for h in (1, -1, NEAR, -NEAR)]
    if nw > 1:
        partners.append(side_mate)
    if ny > 1:
        partners += [up_mate, down_mate]
    barrier = pltpu.get_barrier_semaphore()
    for mate in partners:
        pl.semaphore_signal(barrier, inc=1, device_id=mate, device_id_type=MESH)

    loads = []
    for i, (src, dst) in enumerate(
        (
            (cot_h, cot),
            (feats_h, feats),
            (counts_h, counts),
            (params_h, params),
            (glob_h, glob),
            (first_h, first),
            (second_h, second),
            (mom_h, mom),
        )
    ):
        copy = pltpu.make_async_copy(src, dst, load_sem.at[min(i, 3)])
        copy.start()
        loads.append(copy)

    loads[2].wait()
    live = counts[w]
    live_f = live.astype(F32)
    loads[0].wait()
    position = k * tokens + lax.broadcasted_iota(jnp.int32, cot.shape, 0)
    masked = jnp.where(position < live, cot[...], jnp.zeros_like(cot[...]))
    loads[1].wait()

    def group_z(i):
        return ((z // GROUP + turn(i, groups)) % groups) * GROUP

    def remote(src, dst, send, recv, mate):
        return pltpu.make_async_remote_copy(
            src_ref=src, dst_ref=dst, send_sem=send, recv_sem=recv, device_id=mate, device_id_type=MESH
        )

    core_done, reduced = set(), set()

    def multiply(i):
        base = group_z(i)
        for x in range(2):
            for pair in range(GROUP // 2):
                col = pl.multiple_of((x * zs + base + 2 * pair) * (2 * rows), 4 * rows)
                block = lax.dot_general(
                    feats[:, pl.ds(col, 4 * rows)],
                    masked,
                    (((0,), (0,)), ((), ())),
                    preferred_element_type=F32,
                )
                for dz in range(2):
                    for core in range(2):
                        lo = (2 * dz + core) * rows
                        term[core, x, base + 2 * pair + dz] = block[lo : lo + rows]

    def send_core(i):
        zr = pl.ds(group_z(i), GROUP)
        copy = remote(term.at[1 - c, :, zr], crecv.at[:, zr], csend_sem, crecv_sem.at[part_of(CORE_PARTS, i)], core_mate)
        copy.start()

    far = far_first(steps)

    def z_of(node):
        return (z + node[0] * node[1] + zs) % zs

    def reduce_pair(i):
        part = part_of(CORE_PARTS, i)
        if part not in core_done:
            core_done.add(part)
            wait_core(part)
        zr = pl.ds(group_z(i), GROUP)
        chip[:, zr] = term[c, :, zr] + crecv[:, zr]

    def send_x(i):
        where = groups_of(*far[i], groups)
        for j in range(groups):
            if turn(j, groups) in where and j not in reduced:
                reduced.add(j)
                reduce_pair(j)
        zz = z_of(far[i])
        remote(chip.at[1 - xh, zz], xrecv.at[zz], xsend_sem, xrecv_sem.at[part_of(X_PARTS, i)], x_mate).start()

    def wait_core(part):
        n = GROUP * (CORE_PARTS[part + 1] - CORE_PARTS[part])
        zr = pl.ds(0, n)
        remote(term.at[1 - c, :, zr], crecv.at[:, zr], csend_sem, crecv_sem.at[part], core_mate).wait_recv()

    def wait_x(part):
        zr = pl.ds(0, X_PARTS[part + 1] - X_PARTS[part])
        remote(chip.at[1 - xh, zr], xrecv.at[zr], xsend_sem, xrecv_sem.at[part], x_mate).wait_recv()

    for i in range(groups):
        multiply(i)

    pltpu.make_async_copy(result, result, load_sem.at[3]).wait()
    frag = frag_ref[0]
    old = params[pl.ds(0, rows // FRAGS, stride=FRAGS), :]
    for f in range(1, FRAGS):
        old = jnp.where(frag == f, params[pl.ds(f, rows // FRAGS, stride=FRAGS), :], old)
    mine = live_f * (glob[...] - old)
    drift[...] = mine
    wall[w] = mine

    pl.semaphore_wait(barrier, len(partners))
    for i in range(groups):
        send_core(i)
    for h in (NEAR, -NEAR):
        pl.semaphore_signal(far_sem, inc=1, device_id=z_mate(h), device_id_type=MESH)
    if nw > 1:
        remote(drift, wall.at[w], wsend_sem.at[0], wrecv_sem.at[0], side_mate).start()
    for i in range(zs):
        send_x(i)

    def block(i):
        return wall.at[pl.ds(2 * ((y + i + ny) % ny), 2)]

    def worker_pairs():
        if nw > 1:
            remote(drift, drift, wsend_sem.at[0], wrecv_sem.at[0], side_mate).wait_recv()
        if ny > 1:
            remote(block(0), block(0), wsend_sem.at[1], wrecv_sem.at[1], up_mate).start()
            remote(block(0), block(0), wsend_sem.at[2], wrecv_sem.at[2], down_mate).start()

    def worker_relay():
        if ny > 1:
            remote(block(-1), block(-1), wsend_sem.at[0], wrecv_sem.at[1], up_mate).wait_recv()
            remote(block(-1), block(-1), wsend_sem.at[3], wrecv_sem.at[3], up_mate).start()

    def outer():
        if ny > 1:
            remote(block(1), block(1), wsend_sem.at[0], wrecv_sem.at[2], down_mate).wait_recv()
            remote(block(2), block(2), wsend_sem.at[0], wrecv_sem.at[3], up_mate).wait_recv()
        total = wall[0]
        token_total = counts[0]
        for i in range(1, nw):
            total = total + wall[i]
            token_total = token_total + counts[i]
        pseudo = total / token_total.astype(F32)
        momentum = NESTEROV * mom[...] + pseudo
        fresh = glob[...] - OUTER_RATE * (pseudo + NESTEROV * momentum)
        result[pl.ds(3 * rows + fresh.shape[0], fresh.shape[0]), :] = momentum
        result[pl.ds(3 * rows, fresh.shape[0]), :] = fresh
        for f in range(FRAGS):
            spread[pl.ds(f, rows // FRAGS, stride=FRAGS), :] = fresh

    done = set()

    def need(node):
        part = part_of(X_PARTS, far.index(node))
        if part not in done:
            done.add(part)
            wait_x(part)
            for other in far[X_PARTS[part] : X_PARTS[part + 1]]:
                zz = z_of(other)
                own[zz] = chip[xh, zz] + xrecv[zz]

    def gather(node, zz):
        kin = leaves[node]
        zr = pl.ds(slot[kin[0]], len(kin))
        remote(zrecv.at[zr], zrecv.at[zr], zsend_sem, zrecv_sem.at[channel[node]], x_mate).wait_recv()
        total = own[zz]
        for kid in kin:
            total = total + zrecv[slot[kid]]
        for half in range(2):
            hr = pl.ds(half * (rows // 2), rows // 2)
            part = total[half * (rows // 2) : (half + 1) * (rows // 2)]
            for kid in trunk[node]:
                piece = zrecv.at[slot[kid], hr]
                remote(piece, piece, zsend_sem, zrecv_sem.at[channel[kid, half]], x_mate).wait_recv()
                part = part + zrecv[slot[kid], hr]
            yield hr, half, part

    worker_pairs()
    pl.semaphore_wait(far_sem, 2)
    for count, node in enumerate(order):
        d, o = node
        need(node)
        zz = z_of(node)
        i = slot[node]
        up = (d, o - steps[node]) if o - steps[node] else (0, 0)
        mate = z_mate(d * steps[node])
        if node in kids:
            for hr, half, part in gather(node, zz):
                zsend[i, hr] = part
                sem = zrecv_sem.at[channel[node, half]]
                remote(zsend.at[i, hr], zrecv.at[i, hr], zsend_sem, sem, mate).start()
        else:
            remote(own.at[zz], zrecv.at[i], zsend_sem, zrecv_sem.at[channel[up]], mate).start()
        if count == 4:
            worker_relay()

    need((0, 0))
    outer()
    gradient = jnp.concatenate([part for _, _, part in gather((0, 0), z)]) / live_f
    first_new = BETA_ONE * first[...] + (1.0 - BETA_ONE) * gradient
    second_new = BETA_TWO * second[...] + (1.0 - BETA_TWO) * gradient * gradient
    update = first_new / CORRECT_ONE / (jnp.sqrt(second_new / CORRECT_TWO) + ADAM_EPS)
    before = params[...]
    inner = before - LEARN_RATE * (update + DECAY_RATE * before)
    chosen = lax.broadcasted_iota(jnp.int32, inner.shape, 0) % FRAGS == frag
    result[pl.ds(0, rows), :] = jnp.where(chosen, MIXING * spread[...] + (1.0 - MIXING) * inner, inner)
    result[pl.ds(rows, rows), :] = first_new
    result[pl.ds(2 * rows, rows), :] = second_new

    remote(crecv, crecv, csend_sem, crecv_sem.at[0], core_mate).wait_send()
    remote(xrecv, xrecv, xsend_sem, xrecv_sem.at[0], x_mate).wait_send()
    remote(zrecv, zrecv, zsend_sem, zrecv_sem.at[0], x_mate).wait_send()
    if nw > 1:
        remote(drift, drift, wsend_sem.at[0], wrecv_sem.at[0], side_mate).wait_send()
    for i in range(1, 4 if ny > 1 else 0):
        remote(block(0), block(0), wsend_sem.at[i], wrecv_sem.at[i], up_mate).wait_send()


def hand_out(packed, *refs):
    outs, sems = refs[:-1], refs[-1]
    copies, lo = [], 0
    for i, out in enumerate(outs):
        n = out.shape[0]
        copy = pltpu.make_async_copy(packed.at[pl.ds(lo, n)], out, sems.at[i])
        copy.start()
        copies.append(copy)
        lo += n
    for copy in copies:
        copy.wait()


def solution(mesh):
    nw = mesh.shape["worker"]
    zs = mesh.shape["fsdp"] // 4

    def step(params, first, second, glob, mom, features, cotangent, counts, frag):
        rows, width = params.shape[1:]
        frows = glob.shape[0]
        tokens, depth = features.shape[1:]
        vm = pltpu.VMEM
        dma = pltpu.SemaphoreType.DMA
        messages = zs - 1
        stops = 3 * len(make_order(make_tree(zs), zs)[1])
        groups = zs // GROUP
        tile = (rows, width)
        in_hbm = functools.partial(pltpu.with_memory_space_constraint, memory_space=pltpu.HBM)
        big = jax.ShapeDtypeStruct(tile, F32)
        small = jax.ShapeDtypeStruct((frows, width), F32)
        hbm = pl.BlockSpec(memory_space=pl.ANY)
        packed = pl.pallas_call(
            functools.partial(kernel, nw, zs),
            out_shape=jax.ShapeDtypeStruct((3 * rows + 2 * frows, width), F32),
            in_specs=[hbm, pl.BlockSpec(memory_space=pltpu.SMEM)] + [hbm] * 7,
            out_specs=pl.BlockSpec(memory_space=vm),
            scratch_shapes=[
                pltpu.SMEM((nw,), jnp.int32),
                vm((tokens, depth), jnp.bfloat16),
                vm((tokens, width), jnp.bfloat16),
                vm(tile, F32),
                vm(tile, F32),
                vm(tile, F32),
                vm((frows, width), F32),
                vm((frows, width), F32),
                vm((2, 2, zs) + tile, F32),
                vm((2, zs) + tile, F32),
                vm((2, zs) + tile, F32),
                vm((zs,) + tile, F32),
                vm((zs,) + tile, F32),
                vm((messages,) + tile, F32),
                vm((messages,) + tile, F32),
                vm((frows, width), F32),
                vm((nw, frows, width), F32),
                vm(tile, F32),
                dma((4,)),
                dma(()),
                dma((len(CORE_PARTS) - 1,)),
                dma(()),
                dma((len(X_PARTS) - 1,)),
                dma(()),
                dma((stops,)),
                dma((4,)),
                dma((4,)),
                pltpu.SemaphoreType.REGULAR,
            ],
            compiler_params=pltpu.CompilerParams(collective_id=0, has_side_effects=True, vmem_limit_bytes=VMEM_LIMIT),
            name="diloco_step",
        )(in_hbm(counts), frag, *map(in_hbm, (params[0], first[0], second[0], glob, mom, features[0], cotangent[0])))
        out = pl.pallas_call(
            hand_out,
            out_shape=(big, big, big, small, small),
            in_specs=[hbm],
            out_specs=[hbm] * 5,
            scratch_shapes=[dma((5,))],
            compiler_params=pltpu.CompilerParams(vmem_limit_bytes=1024 * 1024),
            name="hand_out",
        )(packed)
        return (out[0][None], out[1][None], out[2][None], out[3], out[4])

    held = P("worker", "fsdp", None)
    shared = P("fsdp", None)
    return jax.shard_map(
        step,
        mesh=mesh,
        in_specs=(held, held, held, shared, shared, held, held, P(), P()),
        out_specs=(held, held, held, shared, shared),
        check_vma=False,
    )
```
